32 devices in a mesh: seq: 4 (over z), kv: 8 (over y, x, core).
Axes of the slice: x: 2, y: 2, z: 4, core: 2. Of those that a mesh axis runs over, the one named last changes fastest.
Arguments:
- tokens: bfloat16 [4, 1536, 2048], P('seq', 'kv'), may hold values from -6 to 6
- doc_ids: int32 [4, 1536], P('seq', 'kv'), may hold values from 0 to 3, as said below
- w_query: bfloat16 [2048, 2048], P(('seq', 'kv')), may hold values from -0.25 to 0.25
- w_key: bfloat16 [2048, 2048], P(('seq', 'kv')), may hold values from -0.125 to 0.125
- w_value: bfloat16 [2048, 2048], P(('seq', 'kv')), may hold values from -0.125 to 0.125
- w_out: bfloat16 [2048, 2048], P(('seq', 'kv')), may hold values from -0.5 to 0.5
- gain_attn: bfloat16 [2048], P(('seq', 'kv')), may hold values from 0.5 to 1.5
- gain_ffn: bfloat16 [2048], P(('seq', 'kv')), may hold values from 0.5 to 1.5
- w_gate: bfloat16 [2048, 8192], P('seq', 'kv'), may hold values from -0.125 to 0.125
- w_up: bfloat16 [2048, 8192], P('seq', 'kv'), may hold values from -0.125 to 0.125
- w_down: bfloat16 [8192, 2048], P('kv', 'seq'), may hold values from -0.0625 to 0.0625
- cotangent: bfloat16 [4, 1536, 2048], P('seq', 'kv'), may hold values from -6 to 6
Outputs:
- result: bfloat16 [4, 1536, 2048], P('seq', 'kv')
- grad_tokens: float32 [4, 1536, 2048], P('seq', 'kv')
- grad_query: float32 [2048, 2048], P(('seq', 'kv'))
- grad_key: float32 [2048, 2048], P(('seq', 'kv'))
- grad_value: float32 [2048, 2048], P(('seq', 'kv'))
- grad_out: float32 [2048, 2048], P(('seq', 'kv'))
- grad_gain_attn: float32 [2048], P(('seq', 'kv'))
- grad_gain_ffn: float32 [2048], P(('seq', 'kv'))
- grad_gate: float32 [2048, 8192], P('seq', 'kv')
- grad_up: float32 [2048, 8192], P('seq', 'kv')
- grad_down: float32 [8192, 2048], P('kv', 'seq')
- mass_stats: float32 [1], replicated
The draws below stay inside these ranges and needn't reach their ends.
Inputs may be any that keep to these rules, and one draw needn't show every extreme that they name: `doc_ids`: ordered by position pos, the ids of a sequence never fall; each id covers 1 to 768 consecutive positions, and some document has exactly that many.
All inputs are finite; a program needn't handle non-finite values.
Results may differ from the reference program's by a relative error of at most 0.018.
Values may be sent and summed in bfloat16 or wider, within the bound.
No kernel may reach another device: no remote copies, remote signals or barrier semaphores. Data moves between devices by JAX's collectives and lax.ppermute only.
A program may use at most 256 MiB of HBM per device.

```python
import math
from functools import partial
import jax
import jax.numpy as jnp
from jax import lax

D = 2048
HEADS = 16
HEAD_DIM = 128
FF = 8192
TOK_DEV = 192
DOCS = 4
SEQ_LEN = 1536
SEQS = 4


def draw_doc_ids(key, part):
    half_len = SEQ_LEN // 2
    rest = SEQ_LEN - half_len
    local = TOK_DEV
    group = SEQ_LEN // local
    half = local // 2
    rows_index = jnp.arange(SEQ_LEN, dtype=jnp.int32)
    device = rows_index // local
    within = rows_index % local
    positions = jnp.where(within < half, device * half + within, (2 * group - 1 - device) * half + within - half).astype(jnp.int32)

    def one_sequence(seq_key):
        big_key = jax.random.fold_in(seq_key, 11)
        cut_key = jax.random.fold_in(seq_key, 23)
        big = jax.random.randint(big_key, (), 0, DOCS)
        cuts = jnp.sort(jax.random.permutation(cut_key, rest - 1)[:DOCS - 2] + 1).astype(jnp.int32)
        bounds = jnp.concatenate([jnp.zeros((1,), jnp.int32), cuts, jnp.full((1,), rest, jnp.int32)])
        small = bounds[1:] - bounds[:-1]
        index = jnp.arange(DOCS, dtype=jnp.int32)
        before = small[jnp.clip(index, 0, DOCS - 2)]
        after = small[jnp.clip(index - 1, 0, DOCS - 2)]
        lengths = jnp.where(index < big, before, jnp.where(index == big, half_len, after)).astype(jnp.int32)
        ends = jnp.cumsum(lengths)[:DOCS - 1]
        return jnp.sum((positions[:, None] >= ends[None, :]).astype(jnp.int32), axis=1).astype(jnp.int32)
    seq_keys = jax.random.split(jax.random.fold_in(key, 5), SEQS)
    return jax.vmap(one_sequence)(seq_keys)


def shard_levels(own_key, shape, shards, least, largest):
    def one(position, parts):
        draws = jax.random.uniform(jax.random.fold_in(jax.random.fold_in(own_key, 6), position), (parts,), jnp.float32, least / len(shards), largest / len(shards))
        return jnp.repeat(jnp.exp(draws), shape[position] // parts).reshape((-1,) + (1,) * (len(shape) - position - 1))

    level = one(*shards[0])
    for cut in shards[1:]:
        level = level * one(*cut)
    return level


def scatter_about(key, shape, scale, most, cuts=(), kind=jnp.bfloat16):
    values = jax.random.normal(key, shape, jnp.float32) * scale
    if len(cuts) > 0:
        values = shard_levels(key, shape, cuts, -0.22, 0.18) * values
    return jnp.clip(values, min=-most, max=most).astype(kind)


def setup_inputs(seed: int = 0) -> dict:
    splits = jax.random.split(jax.random.key(seed), 13)
    tokens = scatter_about(splits[0], (SEQS, SEQ_LEN, D), 1.0, 6.0, ((0, 4), (1, 8)))
    doc_ids = draw_doc_ids(jax.random.fold_in(splits[12], 71), 0)
    w_query = scatter_about(splits[2], (D, D), (D // 4) ** -0.5, 0.25, ((0, 32),))
    w_key = scatter_about(splits[3], (D, D), D ** -0.5, 0.125, ((0, 32),))
    w_value = scatter_about(splits[4], (D, D), D ** -0.5, 0.125, ((0, 32),))
    w_out = scatter_about(splits[5], (D, D), (D // 16) ** -0.5, 0.5, ((0, 32),))
    gain_attn = jnp.clip(1.0 + 0.1 * jax.random.normal(splits[6], (D,), jnp.float32), 0.5, 1.5).astype(jnp.bfloat16)
    gain_ffn = jnp.clip(1.0 + 0.1 * jax.random.normal(splits[7], (D,), jnp.float32), 0.5, 1.5).astype(jnp.bfloat16)
    w_gate = scatter_about(splits[8], (D, FF), D ** -0.5, 0.125, ((0, 4), (1, 8)))
    w_up = scatter_about(splits[9], (D, FF), D ** -0.5, 0.125, ((0, 4), (1, 8)))
    w_down = scatter_about(splits[10], (FF, D), FF ** -0.5, 0.0625, ((0, 8), (1, 4)))
    cotangent = scatter_about(splits[11], (SEQS, SEQ_LEN, D), 1.0, 6.0, ((0, 4), (1, 8)))
    return {"tokens": tokens, "doc_ids": doc_ids, "w_query": w_query, "w_key": w_key, "w_value": w_value, "w_out": w_out, "gain_attn": gain_attn, "gain_ffn": gain_ffn, "w_gate": w_gate, "w_up": w_up, "w_down": w_down, "cotangent": cotangent}


EPSILON = 1e-05

@jax.custom_vjp
def low(v):
    return lax.optimization_barrier(v.astype(jnp.bfloat16)).astype(jnp.float32)

@jax.custom_vjp
def low_back(v):
    return v

def low_keep(v):
    return (low(v), None)

def low_pass(kept, grad):
    return (grad,)

def back_keep(v):
    return (v, None)

def back_low(kept, grad):
    return (low(grad),)
low.defvjp(low_keep, low_pass)
low_back.defvjp(back_keep, back_low)

def matmul(left, right):
    return jnp.dot(left, right, precision=lax.Precision.HIGHEST)

def rms_norm(values, gain):
    return values * lax.rsqrt(lax.optimization_barrier(jnp.mean(values * values, axis=-1, keepdims=True)) + EPSILON) * gain

def stored_positions(length):
    rows_index = jnp.arange(length, dtype=jnp.int32)
    local = TOK_DEV
    group = length // local
    half = local // 2
    device = rows_index // local
    within = rows_index % local
    return jnp.where(within < half, device * half + within, (2 * group - 1 - device) * half + within - half).astype(jnp.int32)

def rope_tables(length):
    half = HEAD_DIM // 2
    freqs = jnp.exp(jnp.arange(half, dtype=jnp.float32) * (-2.0 * math.log(10000.0) / HEAD_DIM))
    angles = stored_positions(length).astype(jnp.float32)[:, None] * freqs[None, :]
    return (jnp.cos(angles)[:, None, :], jnp.sin(angles)[:, None, :])

def rotate(values, cosine, sine):
    half = values.shape[-1] // 2
    first = values[..., :half]
    second = values[..., half:]
    return jnp.concatenate([first * cosine - second * sine, second * cosine + first * sine], axis=-1)

def attend_sequence(inputs):
    queries, keys, values, ids = inputs
    length = queries.shape[0]
    block = min(512, length)
    count = length // block
    positions = stored_positions(length)
    scale = 1.0 / math.sqrt(HEAD_DIM)
    offset = math.log(length)

    def one_block(pieces):
        q_block, id_block, pos_block = pieces
        scores = jnp.einsum('qhd,khd->hqk', q_block, keys, precision=lax.Precision.HIGHEST) * scale - offset
        scores = low_back(scores)
        allowed = (id_block[:, None] == ids[None, :]) & (pos_block[:, None] >= positions[None, :])
        weights_now = jnp.where(allowed[None], jax.nn.sigmoid(scores), 0.0)
        mass = lax.optimization_barrier(jnp.sum(weights_now, axis=(0, 2)))
        out = jnp.einsum('hqk,khd->qhd', low(weights_now), values, precision=lax.Precision.HIGHEST)
        return (out, mass)
    outs, mass = lax.map(jax.checkpoint(one_block), (queries.reshape(count, block, HEADS, HEAD_DIM), ids.reshape(count, block), positions.reshape(count, block)))
    return (outs.reshape(length, HEADS, HEAD_DIM), mass.reshape(length))

def forward(ids, tokens, w_query, w_key, w_value, w_out, gain_attn, gain_ffn, w_gate, w_up, w_down):
    seqs, length, width = tokens.shape
    flat = tokens.reshape(seqs * length, width)
    normed = low(rms_norm(flat, gain_attn))
    cosine, sine = rope_tables(length)
    shape = (seqs, length, HEADS, HEAD_DIM)
    queries = low(rotate(low_back(matmul(normed, w_query)).reshape(shape), cosine, sine))
    keys = low(rotate(low_back(matmul(normed, w_key)).reshape(shape), cosine, sine))
    values = low_back(low(matmul(normed, w_value))).reshape(shape)
    mixed, mass = lax.map(jax.checkpoint(attend_sequence), (queries, keys, values, ids))
    mixed = low_back(low(mixed.reshape(seqs * length, width)))
    hidden = flat + low_back(matmul(mixed, w_out))
    second = low(rms_norm(hidden, gain_ffn))
    gate = low_back(matmul(second, w_gate))
    up = low_back(matmul(second, w_up))
    inner = low(jax.nn.silu(gate) * up)
    result = hidden + low_back(matmul(inner, w_down))
    return (result.reshape(seqs, length, width), mass)

def reference(tokens, doc_ids, w_query, w_key, w_value, w_out, gain_attn, gain_ffn, w_gate, w_up, w_down, cotangent):
    floats = [item.astype(jnp.float32) for item in (tokens, w_query, w_key, w_value, w_out, gain_attn, gain_ffn, w_gate, w_up, w_down)]
    result, pullback, mass = jax.vjp(partial(forward, doc_ids), *floats, has_aux=True)
    grads = pullback(cotangent.astype(jnp.float32))
    summary = jnp.max(mass).reshape(1)
    return (result.astype(jnp.bfloat16), grads[0], grads[1], grads[2], grads[3], grads[4], grads[5], grads[6], grads[7], grads[8], grads[9], summary)
```

```python
import functools
import math

import jax
import jax.numpy as jnp
from jax import lax
from jax.experimental import pallas as pl
from jax.experimental.pallas import tpu as pltpu
from jax.sharding import PartitionSpec as P

HEAD_DIM = 128
EPSILON = 1e-05
BLOCK = 256
LOG2E = math.log2(math.e)
BF16 = jnp.bfloat16
F32 = jnp.float32


def dot_plain(left, right):
    return jnp.dot(left, right, preferred_element_type=F32)


def dot_left(left, right):
    return lax.dot_general(left, right, (((0,), (0,)), ((), ())), preferred_element_type=F32)


def dot_right(left, right):
    return lax.dot_general(left, right, (((1,), (1,)), ((), ())), preferred_element_type=F32)


def rms_norm(values, gain):
    return values * lax.rsqrt(jnp.mean(values * values, axis=-1, keepdims=True) + EPSILON) * gain


def rms_back(values, gain, grad):
    inverse = lax.rsqrt(jnp.mean(values * values, axis=-1, keepdims=True) + EPSILON)
    scaled = grad * gain
    moment = jnp.mean(values * scaled, axis=-1, keepdims=True)
    return inverse * scaled - values * (inverse * inverse * inverse) * moment


ORDER = (0, 2, 4, 6, 1, 3, 5, 7)


def swap(values, mask):
    size = lax.axis_size("kv")
    return lax.ppermute(values, "kv", [(i, i ^ mask) for i in range(size)])


def owners():
    size = lax.axis_size("kv")
    if size == 8:
        return lax.axis_index("kv").astype(jnp.int32) ^ jnp.array(ORDER, jnp.int32)
    return jnp.arange(size, dtype=jnp.int32)


def gather_chunks(values):
    size = lax.axis_size("kv")
    if size != 8:
        return [lax.all_gather(values, "kv", axis=0, tiled=True)]
    half = values.shape[0] // 2
    near_x = swap(values, 2)
    near_y = swap(values, 4)
    core = swap(values, 1)
    far_top = swap(near_x[:half], 4)
    far_low = swap(near_y[half:], 2)
    core_x = swap(near_x, 1)
    core_y = swap(near_y, 1)
    core_top = swap(far_top, 1)
    core_low = swap(far_low, 1)
    return [values, near_x, near_y, far_top, far_low, core, core_x, core_y, core_top, core_low]


def gather_rows(values):
    return jnp.concatenate(gather_chunks(values), axis=0)


def add16(left, right):
    return (left.astype(F32) + right.astype(F32)).astype(BF16)


def scatter_rows(make):
    size = lax.axis_size("kv")
    if size != 8:
        full = make(0, size)
        return lax.psum_scatter(full, "kv", scatter_dimension=0, tiled=True).astype(F32)
    odd = make(4, 8)
    theirs = swap(odd, 1)
    even = make(0, 4)
    local = even.shape[0] // 4
    half = local // 2

    def both(chunk, low):
        rows = slice(chunk * local + low * half, chunk * local + (low + 1) * half)
        return add16(even[rows], theirs[rows])

    send_x = jnp.concatenate([both(1, 0), both(3, 0)], axis=0)
    send_y = jnp.concatenate([both(2, 1), both(3, 1)], axis=0)
    from_x = swap(send_x, 2)
    from_y = swap(send_y, 4)
    last_y = swap(add16(both(2, 0), from_x[half:]), 4)
    last_x = swap(add16(both(1, 1), from_y[half:]), 2)
    top = both(0, 0).astype(F32) + from_x[:half].astype(F32) + last_y.astype(F32)
    low = both(0, 1).astype(F32) + from_y[:half].astype(F32) + last_x.astype(F32)
    return jnp.concatenate([top, low], axis=0)


def spread_small(values, axis):
    size = lax.axis_size(axis)
    return lax.all_to_all(jnp.broadcast_to(values[None], (size,) + values.shape), axis, 0, 0)


def turn(values, cosine, sine):
    return values * cosine + pltpu.roll(values, HEAD_DIM // 2, 1) * sine


def forward_kernel(
    heads, parts, length, scale, offset,
    source, first, qk_hbm, v_hbm, cos_ref, sin_ref, doc_col, doc_row,
    q_ref, k_ref, v_ref, mass_ref, mixed_hbm,
    qk_s, mixed_s, sems,
):
    wide = heads * HEAD_DIM
    rows = length // parts

    def load(b):
        start = pl.multiple_of(source[b] * rows, rows)
        here = pl.ds(b * rows, rows)
        return (
            pltpu.make_async_copy(qk_hbm.at[pl.ds(start, rows), :], qk_s.at[here, :], sems.at[0, b]),
            pltpu.make_async_copy(v_hbm.at[pl.ds(start, rows), :], v_ref.at[here, :], sems.at[1, b]),
        )

    def store(b):
        start = pl.multiple_of(source[b] * rows, rows)
        return pltpu.make_async_copy(
            mixed_s.at[pl.ds(b * rows, rows), :], mixed_hbm.at[pl.ds(start, rows), :], sems.at[2, b]
        )

    for b in range(parts):
        for copy in load(b):
            copy.start()
    for b in range(parts):
        for copy in load(b):
            copy.wait()

    def rope(b, carry):
        here = pl.ds(pl.multiple_of(b * BLOCK, BLOCK), BLOCK)
        cosine = cos_ref[here, :]
        sine = sin_ref[here, :]
        for h in range(heads):
            lanes = slice(h * HEAD_DIM, (h + 1) * HEAD_DIM)
            more = slice(wide + h * HEAD_DIM, wide + (h + 1) * HEAD_DIM)
            q_ref[here, lanes] = turn(qk_s[here, lanes], cosine, sine).astype(BF16)
            k_ref[here, lanes] = turn(qk_s[here, more], cosine, sine).astype(BF16)
        return carry

    lax.fori_loop(0, length // BLOCK, rope, 0)

    def query_block(i, carry):
        here = pl.ds(pl.multiple_of(i * BLOCK, BLOCK), BLOCK)
        docs = doc_col[here, :]
        row = lax.broadcasted_iota(jnp.int32, (BLOCK, BLOCK), 0)
        col = lax.broadcasted_iota(jnp.int32, (BLOCK, BLOCK), 1)

        def key_block(j, carry):
            accs, mass = carry
            there = pl.ds(pl.multiple_of(j * BLOCK, BLOCK), BLOCK)
            allowed = (docs == doc_row[:, there]) & (row + (i - j) * BLOCK >= col)
            out = []
            for h in range(heads):
                lanes = slice(h * HEAD_DIM, (h + 1) * HEAD_DIM)
                score = dot_right(q_ref[here, lanes], k_ref[there, lanes])
                prob = 1.0 / (1.0 + jnp.exp2(score * (-scale * LOG2E) + offset * LOG2E))
                prob = jnp.where(allowed, prob, 0.0)
                for part in range(BLOCK // 128):
                    mass = mass + prob[:, part * 128 : (part + 1) * 128]
                out.append(accs[h] + dot_plain(prob.astype(BF16), v_ref[there, lanes]))
            return (tuple(out), mass)

        zero = jnp.zeros((BLOCK, HEAD_DIM), F32)
        accs, mass = lax.fori_loop(first[i], i + 1, key_block, ((zero,) * heads, zero))
        for h in range(heads):
            mixed_s[here, h * HEAD_DIM : (h + 1) * HEAD_DIM] = accs[h].astype(BF16)
        mass_ref[here, :] = jnp.sum(mass, axis=1, keepdims=True)
        return carry

    lax.fori_loop(0, length // BLOCK, query_block, 0)
    for b in range(parts):
        store(b).start()
    for b in range(parts):
        store(b).wait()


def attend_forward(source, first, qk, v, cosine, sine, doc_col, doc_row):
    length, wide = v.shape
    heads = wide // HEAD_DIM
    parts = source.shape[0]
    vmem = pl.BlockSpec(memory_space=pltpu.VMEM)
    smem = pl.BlockSpec(memory_space=pltpu.SMEM)
    hbm = pl.BlockSpec(memory_space=pl.ANY)
    same = jax.ShapeDtypeStruct((length, wide), BF16)
    return pl.pallas_call(
        functools.partial(
            forward_kernel, heads, parts, length, 1.0 / math.sqrt(HEAD_DIM), math.log(length)
        ),
        name="attend_forward",
        out_shape=(same, same, same, jax.ShapeDtypeStruct((length, 1), F32), same),
        in_specs=[smem, smem, hbm, hbm, vmem, vmem, vmem, vmem],
        out_specs=(vmem, vmem, vmem, vmem, hbm),
        scratch_shapes=[
            pltpu.VMEM((length, 2 * wide), F32),
            pltpu.VMEM((length, wide), BF16),
            pltpu.SemaphoreType.DMA((3, parts)),
        ],
        cost_estimate=pl.CostEstimate(
            flops=2 * length * length * wide,
            transcendentals=length * length * heads,
            bytes_accessed=length * wide * 18,
        ),
    )(source, first, qk, v, cosine, sine, doc_col, doc_row)


def backward_kernel(
    heads, parts, length, scale, offset,
    source, last, q_ref, k_ref, v_ref, g_hbm, cos_ref, sin_ref, doc_col, doc_row,
    out_hbm,
    g_s, dq_s, out_s, sems,
):
    wide = heads * HEAD_DIM
    rows = length // parts

    def load(b):
        start = pl.multiple_of(source[b] * rows, rows)
        return pltpu.make_async_copy(
            g_hbm.at[pl.ds(start, rows), :], g_s.at[pl.ds(b * rows, rows), :], sems.at[0, b]
        )

    def store(b):
        start = pl.multiple_of(source[b] * rows, rows)
        return pltpu.make_async_copy(
            out_s.at[pl.ds(b * rows, rows), :], out_hbm.at[pl.ds(start, rows), :], sems.at[1, b]
        )

    for b in range(parts):
        load(b).start()
    dq_s[...] = jnp.zeros_like(dq_s)
    for b in range(parts):
        load(b).wait()

    def key_block(j, carry):
        there = pl.ds(pl.multiple_of(j * BLOCK, BLOCK), BLOCK)
        docs = doc_col[there, :]
        row = lax.broadcasted_iota(jnp.int32, (BLOCK, BLOCK), 0)
        col = lax.broadcasted_iota(jnp.int32, (BLOCK, BLOCK), 1)

        def query_block(i, carry):
            dks, dvs = carry
            here = pl.ds(pl.multiple_of(i * BLOCK, BLOCK), BLOCK)
            allowed = (docs == doc_row[:, here]) & (col + (i - j) * BLOCK >= row)
            new_k, new_v = [], []
            for h in range(heads):
                lanes = slice(h * HEAD_DIM, (h + 1) * HEAD_DIM)
                query = q_ref[here, lanes]
                grad = g_s[here, lanes]
                score = dot_right(k_ref[there, lanes], query)
                prob = 1.0 / (1.0 + jnp.exp2(score * (-scale * LOG2E) + offset * LOG2E))
                prob = jnp.where(allowed, prob, 0.0)
                new_v.append(dvs[h] + dot_plain(prob.astype(BF16), grad))
                dprob = dot_right(v_ref[there, lanes], grad)
                dscore = (dprob * (prob - prob * prob)).astype(BF16)
                new_k.append(dks[h] + dot_plain(dscore, query))
                dq_s[here, lanes] += dot_left(dscore, k_ref[there, lanes])
            return (tuple(new_k), tuple(new_v))

        zero = (jnp.zeros((BLOCK, HEAD_DIM), F32),) * heads
        dks, dvs = lax.fori_loop(j, last[j], query_block, (zero, zero))
        cosine = cos_ref[there, :]
        sine = sin_ref[there, :]
        for h in range(heads):
            lanes = slice(h * HEAD_DIM, (h + 1) * HEAD_DIM)
            more = slice(wide + h * HEAD_DIM, wide + (h + 1) * HEAD_DIM)
            most = slice(2 * wide + h * HEAD_DIM, 2 * wide + (h + 1) * HEAD_DIM)
            out_s[there, lanes] = turn(dq_s[there, lanes] * scale, cosine, -sine).astype(BF16)
            out_s[there, more] = turn(dks[h] * scale, cosine, -sine).astype(BF16)
            out_s[there, most] = dvs[h].astype(BF16)
        return carry

    lax.fori_loop(0, length // BLOCK, key_block, 0)
    for b in range(parts):
        store(b).start()
    for b in range(parts):
        store(b).wait()


def attend_backward(source, last, q, k, v, grad, cosine, sine, doc_col, doc_row):
    length, wide = v.shape
    heads = wide // HEAD_DIM
    parts = source.shape[0]
    vmem = pl.BlockSpec(memory_space=pltpu.VMEM)
    smem = pl.BlockSpec(memory_space=pltpu.SMEM)
    hbm = pl.BlockSpec(memory_space=pl.ANY)
    return pl.pallas_call(
        functools.partial(
            backward_kernel, heads, parts, length, 1.0 / math.sqrt(HEAD_DIM), math.log(length)
        ),
        name="attend_backward",
        out_shape=jax.ShapeDtypeStruct((length, 3 * wide), BF16),
        in_specs=[smem, smem, vmem, vmem, vmem, hbm, vmem, vmem, vmem, vmem],
        out_specs=hbm,
        scratch_shapes=[
            pltpu.VMEM((length, wide), BF16),
            pltpu.VMEM((length, wide), F32),
            pltpu.VMEM((length, 3 * wide), BF16),
            pltpu.SemaphoreType.DMA((2, parts)),
        ],
        cost_estimate=pl.CostEstimate(
            flops=5 * length * length * wide,
            transcendentals=length * length * heads,
            bytes_accessed=length * wide * 14,
        ),
    )(source, last, q, k, v, grad, cosine, sine, doc_col, doc_row)


def per_device(
    tokens,
    doc_ids,
    w_query,
    w_key,
    w_value,
    w_out,
    gain_attn,
    gain_ffn,
    w_gate,
    w_up,
    w_down,
    cotangent,
):
    ring = lax.axis_size("seq")
    group = lax.axis_size("kv")
    seqs, local, width = tokens.shape
    length = local * group
    piece = w_query.shape[0]
    heads = width // HEAD_DIM
    planes = heads // ring
    share = group // planes
    mine = ring // share
    wide = mine * HEAD_DIM
    pairs = [[j * share + c for c in range(share)] for j in range(planes)]

    def chunk_rows(values, start, stop):
        return values[start * local : stop * local]

    flat16 = tokens.reshape(local, width)
    flat = flat16.astype(F32)
    dy16 = cotangent.reshape(local, width)

    gate_w = lax.all_gather(w_gate, "seq", axis=0, tiled=True)
    w_three = jnp.stack([w_query, w_key, w_value])
    w_three = w_three.reshape(3, piece, share, mine, planes, HEAD_DIM)
    w_three = w_three.transpose(4, 2, 1, 0, 3, 5).reshape(group, piece, 3 * wide)
    w_three = lax.all_to_all(w_three, "kv", 0, 0).reshape(group * piece, 3 * wide)
    w_three = lax.all_gather(w_three, "seq", axis=0, tiled=True)
    out_w = lax.all_gather(w_out, "seq", axis=0, tiled=False)
    out_w = lax.all_to_all(
        out_w.reshape(share, mine, piece, width), "kv", 0, 0, axis_index_groups=pairs
    )
    out_w = out_w.transpose(1, 0, 2, 3).reshape(wide, width)
    up_w = lax.all_gather(w_up, "seq", axis=0, tiled=True)
    down_w = lax.all_gather(w_down, "seq", axis=1, tiled=True)

    gains = spread_small(spread_small(jnp.stack([gain_attn, gain_ffn]), "kv"), "seq")
    gains = gains.transpose(2, 0, 1, 3).reshape(2, width).astype(F32)
    ids = spread_small(doc_ids.reshape(local), "kv")

    half = local // 2
    by_pos = jnp.concatenate([ids[:, :half], ids[::-1, half:]], axis=0).reshape(length)
    blocks = length // BLOCK
    starts = by_pos.reshape(blocks, BLOCK)[:, 0]
    ends = by_pos.reshape(blocks, BLOCK)[:, -1]
    first = jnp.sum((by_pos[None] < starts[:, None]).astype(jnp.int32), axis=1) // BLOCK
    last = (jnp.sum((by_pos[None] <= ends[:, None]).astype(jnp.int32), axis=1) + BLOCK - 1) // BLOCK
    doc_col = by_pos.reshape(length, 1)
    doc_row = by_pos.reshape(1, length)
    order = jnp.argsort(owners()).astype(jnp.int32) if group != 8 else None
    if group == 8:
        where = [ORDER.index(m) for m in range(8)]
        order = jnp.array(where, jnp.int32)[
            lax.axis_index("kv").astype(jnp.int32) ^ jnp.arange(8, dtype=jnp.int32)
        ]
    source = jnp.concatenate([2 * order, 2 * order[::-1] + 1])

    angle = jnp.arange(length, dtype=F32)[:, None] * jnp.exp(
        jnp.arange(HEAD_DIM // 2, dtype=F32) * (-2.0 * math.log(10000.0) / HEAD_DIM)
    )
    cosine = jnp.cos(angle)
    sine = jnp.sin(angle)
    cosine = jnp.concatenate([cosine, cosine], axis=1)
    sine = jnp.concatenate([-sine, sine], axis=1)

    all_tokens = gather_rows(flat16)
    normed = rms_norm(all_tokens.astype(F32), gains[0]).astype(BF16)
    qk = dot_plain(normed, w_three[:, : 2 * wide])
    v = dot_plain(normed, w_three[:, 2 * wide :]).astype(BF16)
    q, k, v, mass, mixed = attend_forward(source, first, qk, v, cosine, sine, doc_col, doc_row)

    def partial_hidden(start, stop):
        return dot_plain(chunk_rows(mixed, start, stop), out_w).astype(BF16)

    hidden = flat + scatter_rows(partial_hidden)
    masses = lax.all_to_all(mass.reshape(group, local), "kv", 0, 0)
    peak = jnp.max(jnp.sum(masses, axis=0)).reshape(1)
    peak = jnp.max(spread_small(peak, "kv")).reshape(1)
    summary = jnp.max(spread_small(peak, "seq")).reshape(1)

    second16 = rms_norm(hidden, gains[1]).astype(BF16)
    dy_all = gather_rows(dy16)
    second_all = gather_rows(second16)
    gate = dot_plain(second_all, gate_w)
    up = dot_plain(second_all, up_w)
    gate_sigmoid = jax.nn.sigmoid(gate)
    swish = gate * gate_sigmoid
    inner = (swish * up).astype(BF16)
    grad_down = dot_left(dy_all, inner).astype(BF16)
    grads_down = lax.psum_scatter(grad_down, "seq", scatter_dimension=0, tiled=True)
    grad_inner = dot_right(dy_all, down_w)
    dgate = (grad_inner * up * (gate_sigmoid * (1.0 + gate * (1.0 - gate_sigmoid)))).astype(BF16)
    dup = (grad_inner * swish).astype(BF16)

    def partial_second(start, stop):
        return (
            dot_right(chunk_rows(dgate, start, stop), gate_w)
            + dot_right(chunk_rows(dup, start, stop), up_w)
        ).astype(BF16)

    grad_second = scatter_rows(partial_second)
    grads_gate = lax.psum_scatter(
        dot_left(second_all, dgate).astype(BF16), "seq", scatter_dimension=0, tiled=True
    ).astype(F32)
    grads_up = lax.psum_scatter(
        dot_left(second_all, dup).astype(BF16), "seq", scatter_dimension=0, tiled=True
    ).astype(F32)
    grads_down = grads_down.astype(F32).T

    def partial_result(start, stop):
        return dot_plain(chunk_rows(inner, start, stop), down_w).astype(BF16)

    result = hidden + scatter_rows(partial_result)

    grad_hidden = dy16.astype(F32) + rms_back(hidden, gains[1], grad_second)
    dh_all = gather_rows(grad_hidden.astype(BF16))
    dmixed = dot_right(dh_all, out_w).astype(BF16)
    grad_w_out = dot_left(mixed, dh_all).astype(BF16)
    dqkv = attend_backward(source, last, q, k, v, dmixed, cosine, sine, doc_col, doc_row)

    def partial_normed(start, stop):
        return dot_right(chunk_rows(dqkv, start, stop), w_three).astype(BF16)

    grad_normed = scatter_rows(partial_normed)
    grad_input = grad_hidden + rms_back(flat, gains[0], grad_normed)

    grad_w_out = grad_w_out.reshape(mine, share, piece, width).transpose(1, 0, 2, 3)
    grad_w_out = lax.all_to_all(grad_w_out, "kv", 0, 0, axis_index_groups=pairs)
    grad_w_out = lax.psum_scatter(
        grad_w_out.reshape(ring * piece, width), "seq", scatter_dimension=0, tiled=True
    ).astype(F32)
    grad_three = lax.psum_scatter(
        dot_left(normed, dqkv).astype(BF16), "seq", scatter_dimension=0, tiled=True
    )
    grad_three = lax.all_to_all(grad_three.reshape(group, piece, 3 * wide), "kv", 0, 0)
    grad_three = grad_three.reshape(planes, share, piece, 3, mine, HEAD_DIM)
    grad_three = grad_three.transpose(3, 2, 1, 4, 0, 5).reshape(3, piece, width).astype(F32)

    grad_gain1 = jnp.sum(
        w_query.astype(F32) * grad_three[0]
        + w_key.astype(F32) * grad_three[1]
        + w_value.astype(F32) * grad_three[2],
        axis=1,
    ) / gain_attn.astype(F32)
    part2 = jnp.sum(w_gate.astype(F32) * grads_gate + w_up.astype(F32) * grads_up, axis=1)
    part2 = lax.all_to_all(part2.reshape(group, -1), "kv", 0, 0)
    grad_gain2 = jnp.sum(part2, axis=0) / gain_ffn.astype(F32)

    return (
        result.reshape(seqs, local, width).astype(BF16),
        grad_input.reshape(seqs, local, width),
        grad_three[0],
        grad_three[1],
        grad_three[2],
        grad_w_out,
        grad_gain1,
        grad_gain2,
        grads_gate,
        grads_up,
        grads_down,
        summary,
    )


def solution(mesh):
    tokens = P("seq", "kv", None)
    rows = P(("seq", "kv"), None)
    vector = P(("seq", "kv"))
    grid = P("seq", "kv")
    in_specs = (
        tokens, P("seq", "kv"), rows, rows, rows, rows, vector, vector, grid, grid,
        P("kv", "seq"), tokens,
    )
    out_specs = (
        tokens, tokens, rows, rows, rows, rows, vector, vector, grid, grid, P("kv", "seq"), P(),
    )
    return jax.shard_map(
        per_device, mesh=mesh, in_specs=in_specs, out_specs=out_specs, check_vma=False
    )
```

```python
import functools
import math

import jax
import jax.numpy as jnp
from jax import lax
from jax.experimental import pallas as pl
from jax.experimental.pallas import tpu as pltpu
from jax.sharding import PartitionSpec as P

HEAD_DIM = 128
EPSILON = 1e-05
BLOCK = 256
LOG2E = math.log2(math.e)
BF16 = jnp.bfloat16
F32 = jnp.float32


def dot_plain(left, right):
    return jnp.dot(left, right, preferred_element_type=F32)


def dot_left(left, right):
    return lax.dot_general(left, right, (((0,), (0,)), ((), ())), preferred_element_type=F32)


def dot_right(left, right):
    return lax.dot_general(left, right, (((1,), (1,)), ((), ())), preferred_element_type=F32)


def rms_norm(values, gain):
    return values * lax.rsqrt(jnp.mean(values * values, axis=-1, keepdims=True) + EPSILON) * gain


def rms_back(values, gain, grad):
    inverse = lax.rsqrt(jnp.mean(values * values, axis=-1, keepdims=True) + EPSILON)
    scaled = grad * gain
    moment = jnp.mean(values * scaled, axis=-1, keepdims=True)
    return inverse * scaled - values * (inverse * inverse * inverse) * moment


def gain_rows(values, grad):
    inverse = lax.rsqrt(jnp.mean(values * values, axis=-1, keepdims=True) + EPSILON)
    return jnp.sum(grad * values * inverse, axis=0)


ORDER = (0, 2, 4, 6, 1, 3, 5, 7)


def swap(values, mask):
    size = lax.axis_size("kv")
    return lax.ppermute(values, "kv", [(i, i ^ mask) for i in range(size)])


def owners():
    size = lax.axis_size("kv")
    if size == 8:
        return lax.axis_index("kv").astype(jnp.int32) ^ jnp.array(ORDER, jnp.int32)
    return jnp.arange(size, dtype=jnp.int32)


def gather_chunks(values):
    size = lax.axis_size("kv")
    if size != 8:
        return [lax.all_gather(values, "kv", axis=0, tiled=True)]
    half = values.shape[0] // 2
    near_x = swap(values, 2)
    near_y = swap(values, 4)
    core = swap(values, 1)
    far_top = swap(near_x[:half], 4)
    far_low = swap(near_y[half:], 2)
    core_x = swap(near_x, 1)
    core_y = swap(near_y, 1)
    core_top = swap(far_top, 1)
    core_low = swap(far_low, 1)
    return [values, near_x, near_y, far_top, far_low, core, core_x, core_y, core_top, core_low]


def gather_rows(values):
    return jnp.concatenate(gather_chunks(values), axis=0)


def add16(left, right):
    return (left.astype(F32) + right.astype(F32)).astype(BF16)


def scatter_rows(make):
    size = lax.axis_size("kv")
    if size != 8:
        full = make(0, size)
        return lax.psum_scatter(full, "kv", scatter_dimension=0, tiled=True).astype(F32)
    odd = make(4, 8)
    theirs = swap(odd, 1)
    even = make(0, 4)
    local = even.shape[0] // 4
    half = local // 2

    def both(chunk, low):
        rows = slice(chunk * local + low * half, chunk * local + (low + 1) * half)
        return add16(even[rows], theirs[rows])

    send_x, send_y = lax.optimization_barrier(
        (
            jnp.concatenate([both(1, 0), both(3, 0)], axis=0),
            jnp.concatenate([both(2, 1), both(3, 1)], axis=0),
        )
    )
    from_x, from_y = lax.optimization_barrier((swap(send_x, 2), swap(send_y, 4)))
    send_y, send_x = lax.optimization_barrier(
        (add16(both(2, 0), from_x[half:]), add16(both(1, 1), from_y[half:]))
    )
    last_y, last_x = lax.optimization_barrier((swap(send_y, 4), swap(send_x, 2)))
    top = both(0, 0).astype(F32) + from_x[:half].astype(F32) + last_y.astype(F32)
    low = both(0, 1).astype(F32) + from_y[:half].astype(F32) + last_x.astype(F32)
    return jnp.concatenate([top, low], axis=0)


def after(values, *others):
    return lax.optimization_barrier((values,) + tuple(others))[0]


def exchange(values):
    size = lax.axis_size("kv")
    if size != 8:
        return lax.all_to_all(values, "kv", 0, 0)
    index = lax.axis_index("kv").astype(jnp.int32)
    relative = index ^ jnp.arange(size, dtype=jnp.int32)
    ordered = values[relative]
    moved = jnp.stack([ordered[0]] + [swap(ordered[m], m) for m in range(1, size)])
    return moved[relative]


def spread_small(values, axis):
    size = lax.axis_size(axis)
    return lax.all_to_all(jnp.broadcast_to(values[None], (size,) + values.shape), axis, 0, 0)


def turn(values, cosine, sine):
    return values * cosine + pltpu.roll(values, HEAD_DIM // 2, 1) * sine


def forward_kernel(
    heads, parts, length, scale, offset,
    source, first, qk_hbm, v_hbm, cos_ref, sin_ref, doc_col, doc_row,
    q_ref, k_ref, v_ref, mass_ref, mixed_hbm,
    qk_s, mixed_s, sems,
):
    wide = heads * HEAD_DIM
    rows = length // parts

    def load(b):
        start = pl.multiple_of(source[b] * rows, rows)
        here = pl.ds(b * rows, rows)
        return (
            pltpu.make_async_copy(qk_hbm.at[pl.ds(start, rows), :], qk_s.at[here, :], sems.at[0, b]),
            pltpu.make_async_copy(v_hbm.at[pl.ds(start, rows), :], v_ref.at[here, :], sems.at[1, b]),
        )

    def store(b):
        start = pl.multiple_of(source[b] * rows, rows)
        return pltpu.make_async_copy(
            mixed_s.at[pl.ds(b * rows, rows), :], mixed_hbm.at[pl.ds(start, rows), :], sems.at[2, b]
        )

    for b in range(parts):
        for copy in load(b):
            copy.start()
    for b in range(parts):
        for copy in load(b):
            copy.wait()

    def rope(b, carry):
        here = pl.ds(pl.multiple_of(b * BLOCK, BLOCK), BLOCK)
        cosine = cos_ref[here, :]
        sine = sin_ref[here, :]
        for h in range(heads):
            lanes = slice(h * HEAD_DIM, (h + 1) * HEAD_DIM)
            more = slice(wide + h * HEAD_DIM, wide + (h + 1) * HEAD_DIM)
            q_ref[here, lanes] = turn(qk_s[here, lanes], cosine, sine).astype(BF16)
            k_ref[here, lanes] = turn(qk_s[here, more], cosine, sine).astype(BF16)
        return carry

    lax.fori_loop(0, length // BLOCK, rope, 0)

    def query_block(i, carry):
        here = pl.ds(pl.multiple_of(i * BLOCK, BLOCK), BLOCK)
        docs = doc_col[here, :]
        row = lax.broadcasted_iota(jnp.int32, (BLOCK, BLOCK), 0)
        col = lax.broadcasted_iota(jnp.int32, (BLOCK, BLOCK), 1)

        def key_block(j, carry):
            accs, mass = carry
            there = pl.ds(pl.multiple_of(j * BLOCK, BLOCK), BLOCK)
            allowed = (docs == doc_row[:, there]) & (row + (i - j) * BLOCK >= col)
            out = []
            for h in range(heads):
                lanes = slice(h * HEAD_DIM, (h + 1) * HEAD_DIM)
                score = dot_right(q_ref[here, lanes], k_ref[there, lanes])
                prob = 1.0 / (1.0 + jnp.exp2(score * (-scale * LOG2E) + offset * LOG2E))
                prob = jnp.where(allowed, prob, 0.0)
                for part in range(BLOCK // 128):
                    mass = mass + prob[:, part * 128 : (part + 1) * 128]
                out.append(accs[h] + dot_plain(prob.astype(BF16), v_ref[there, lanes]))
            return (tuple(out), mass)

        zero = jnp.zeros((BLOCK, HEAD_DIM), F32)
        accs, mass = lax.fori_loop(first[i], i + 1, key_block, ((zero,) * heads, zero))
        for h in range(heads):
            mixed_s[here, h * HEAD_DIM : (h + 1) * HEAD_DIM] = accs[h].astype(BF16)
        mass_ref[here, :] = jnp.sum(mass, axis=1, keepdims=True)
        return carry

    lax.fori_loop(0, length // BLOCK, query_block, 0)
    for b in range(parts):
        store(b).start()
    for b in range(parts):
        store(b).wait()


def attend_forward(source, first, qk, v, cosine, sine, doc_col, doc_row):
    length, wide = v.shape
    heads = wide // HEAD_DIM
    parts = source.shape[0]
    vmem = pl.BlockSpec(memory_space=pltpu.VMEM)
    smem = pl.BlockSpec(memory_space=pltpu.SMEM)
    hbm = pl.BlockSpec(memory_space=pl.ANY)
    same = jax.ShapeDtypeStruct((length, wide), BF16)
    return pl.pallas_call(
        functools.partial(
            forward_kernel, heads, parts, length, 1.0 / math.sqrt(HEAD_DIM), math.log(length)
        ),
        name="attend_forward",
        out_shape=(same, same, same, jax.ShapeDtypeStruct((length, 1), F32), same),
        in_specs=[smem, smem, hbm, hbm, vmem, vmem, vmem, vmem],
        out_specs=(vmem, vmem, vmem, vmem, hbm),
        scratch_shapes=[
            pltpu.VMEM((length, 2 * wide), F32),
            pltpu.VMEM((length, wide), BF16),
            pltpu.SemaphoreType.DMA((3, parts)),
        ],
        cost_estimate=pl.CostEstimate(
            flops=2 * length * length * wide,
            transcendentals=length * length * heads,
            bytes_accessed=length * wide * 18,
        ),
    )(source, first, qk, v, cosine, sine, doc_col, doc_row)


def backward_kernel(
    heads, parts, length, scale, offset,
    source, last, q_ref, k_ref, v_ref, g_hbm, cos_ref, sin_ref, doc_col, doc_row,
    out_hbm,
    g_s, dq_s, out_s, sems,
):
    wide = heads * HEAD_DIM
    rows = length // parts

    def load(b):
        start = pl.multiple_of(source[b] * rows, rows)
        return pltpu.make_async_copy(
            g_hbm.at[pl.ds(start, rows), :], g_s.at[pl.ds(b * rows, rows), :], sems.at[0, b]
        )

    def store(b):
        start = pl.multiple_of(source[b] * rows, rows)
        return pltpu.make_async_copy(
            out_s.at[pl.ds(b * rows, rows), :], out_hbm.at[pl.ds(start, rows), :], sems.at[1, b]
        )

    for b in range(parts):
        load(b).start()
    dq_s[...] = jnp.zeros_like(dq_s)
    for b in range(parts):
        load(b).wait()

    def key_block(j, carry):
        there = pl.ds(pl.multiple_of(j * BLOCK, BLOCK), BLOCK)
        docs = doc_col[there, :]
        row = lax.broadcasted_iota(jnp.int32, (BLOCK, BLOCK), 0)
        col = lax.broadcasted_iota(jnp.int32, (BLOCK, BLOCK), 1)

        def query_block(i, carry):
            dks, dvs = carry
            here = pl.ds(pl.multiple_of(i * BLOCK, BLOCK), BLOCK)
            allowed = (docs == doc_row[:, here]) & (col + (i - j) * BLOCK >= row)
            new_k, new_v = [], []
            for h in range(heads):
                lanes = slice(h * HEAD_DIM, (h + 1) * HEAD_DIM)
                query = q_ref[here, lanes]
                grad = g_s[here, lanes]
                score = dot_right(k_ref[there, lanes], query)
                prob = 1.0 / (1.0 + jnp.exp2(score * (-scale * LOG2E) + offset * LOG2E))
                prob = jnp.where(allowed, prob, 0.0)
                new_v.append(dvs[h] + dot_plain(prob.astype(BF16), grad))
                dprob = dot_right(v_ref[there, lanes], grad)
                dscore = (dprob * (prob - prob * prob)).astype(BF16)
                new_k.append(dks[h] + dot_plain(dscore, query))
                dq_s[here, lanes] += dot_left(dscore, k_ref[there, lanes])
            return (tuple(new_k), tuple(new_v))

        zero = (jnp.zeros((BLOCK, HEAD_DIM), F32),) * heads
        dks, dvs = lax.fori_loop(j, last[j], query_block, (zero, zero))
        cosine = cos_ref[there, :]
        sine = sin_ref[there, :]
        for h in range(heads):
            lanes = slice(h * HEAD_DIM, (h + 1) * HEAD_DIM)
            more = slice(wide + h * HEAD_DIM, wide + (h + 1) * HEAD_DIM)
            most = slice(2 * wide + h * HEAD_DIM, 2 * wide + (h + 1) * HEAD_DIM)
            out_s[there, lanes] = turn(dq_s[there, lanes] * scale, cosine, -sine).astype(BF16)
            out_s[there, more] = turn(dks[h] * scale, cosine, -sine).astype(BF16)
            out_s[there, most] = dvs[h].astype(BF16)
        return carry

    lax.fori_loop(0, length // BLOCK, key_block, 0)
    for b in range(parts):
        store(b).start()
    for b in range(parts):
        store(b).wait()


def attend_backward(source, last, q, k, v, grad, cosine, sine, doc_col, doc_row):
    length, wide = v.shape
    heads = wide // HEAD_DIM
    parts = source.shape[0]
    vmem = pl.BlockSpec(memory_space=pltpu.VMEM)
    smem = pl.BlockSpec(memory_space=pltpu.SMEM)
    hbm = pl.BlockSpec(memory_space=pl.ANY)
    return pl.pallas_call(
        functools.partial(
            backward_kernel, heads, parts, length, 1.0 / math.sqrt(HEAD_DIM), math.log(length)
        ),
        name="attend_backward",
        out_shape=jax.ShapeDtypeStruct((length, 3 * wide), BF16),
        in_specs=[smem, smem, vmem, vmem, vmem, hbm, vmem, vmem, vmem, vmem],
        out_specs=hbm,
        scratch_shapes=[
            pltpu.VMEM((length, wide), BF16),
            pltpu.VMEM((length, wide), F32),
            pltpu.VMEM((length, 3 * wide), BF16),
            pltpu.SemaphoreType.DMA((2, parts)),
        ],
        cost_estimate=pl.CostEstimate(
            flops=5 * length * length * wide,
            transcendentals=length * length * heads,
            bytes_accessed=length * wide * 14,
        ),
    )(source, last, q, k, v, grad, cosine, sine, doc_col, doc_row)


def per_device(
    tokens,
    doc_ids,
    w_query,
    w_key,
    w_value,
    w_out,
    gain_attn,
    gain_ffn,
    w_gate,
    w_up,
    w_down,
    cotangent,
):
    ring = lax.axis_size("seq")
    group = lax.axis_size("kv")
    seqs, local, width = tokens.shape
    length = local * group
    piece = w_query.shape[0]
    heads = width // HEAD_DIM
    planes = heads // ring
    share = group // planes
    mine = ring // share
    wide = mine * HEAD_DIM
    pairs = [[j * share + c for c in range(share)] for j in range(planes)]

    def chunk_rows(values, start, stop):
        return values[start * local : stop * local]

    flat16 = tokens.reshape(local, width)
    flat = flat16.astype(F32)
    dy16 = cotangent.reshape(local, width)

    w_three = jnp.stack([w_query, w_key, w_value])
    w_three = w_three.reshape(3, piece, share, mine, planes, HEAD_DIM)
    w_three = w_three.transpose(4, 2, 1, 0, 3, 5).reshape(group, piece, 3 * wide)
    w_three = exchange(w_three).reshape(group * piece, 3 * wide)
    w_three = lax.all_gather(w_three, "seq", axis=0, tiled=True)
    out_w = lax.all_gather(w_out, "seq", axis=0, tiled=False)
    out_w = lax.all_to_all(
        out_w.reshape(share, mine, piece, width), "kv", 0, 0, axis_index_groups=pairs
    )
    out_w = out_w.transpose(1, 0, 2, 3).reshape(wide, width)
    gate_w = lax.all_gather(w_gate, "seq", axis=0, tiled=True)
    up_w = lax.all_gather(w_up, "seq", axis=0, tiled=True)
    down_w = lax.all_gather(w_down, "seq", axis=1, tiled=True)

    gains = spread_small(spread_small(jnp.stack([gain_attn, gain_ffn]), "kv"), "seq")
    gains = gains.transpose(2, 0, 1, 3).reshape(2, width).astype(F32)
    ids = spread_small(doc_ids.reshape(local), "kv")

    half = local // 2
    by_pos = jnp.concatenate([ids[:, :half], ids[::-1, half:]], axis=0).reshape(length)
    blocks = length // BLOCK
    starts = by_pos.reshape(blocks, BLOCK)[:, 0]
    ends = by_pos.reshape(blocks, BLOCK)[:, -1]
    first = jnp.sum((by_pos[None] < starts[:, None]).astype(jnp.int32), axis=1) // BLOCK
    last = (jnp.sum((by_pos[None] <= ends[:, None]).astype(jnp.int32), axis=1) + BLOCK - 1) // BLOCK
    doc_col = by_pos.reshape(length, 1)
    doc_row = by_pos.reshape(1, length)
    order = jnp.argsort(owners()).astype(jnp.int32) if group != 8 else None
    if group == 8:
        where = [ORDER.index(m) for m in range(8)]
        order = jnp.array(where, jnp.int32)[
            lax.axis_index("kv").astype(jnp.int32) ^ jnp.arange(8, dtype=jnp.int32)
        ]
    source = jnp.concatenate([2 * order, 2 * order[::-1] + 1])

    angle = jnp.arange(length, dtype=F32)[:, None] * jnp.exp(
        jnp.arange(HEAD_DIM // 2, dtype=F32) * (-2.0 * math.log(10000.0) / HEAD_DIM)
    )
    cosine = jnp.cos(angle)
    sine = jnp.sin(angle)
    cosine = jnp.concatenate([cosine, cosine], axis=1)
    sine = jnp.concatenate([-sine, sine], axis=1)

    token_chunks = gather_chunks(flat16)
    all_tokens = jnp.concatenate(token_chunks, axis=0)
    dy_chunks = gather_chunks(after(dy16, *token_chunks[-2:]))
    dy_all = jnp.concatenate(dy_chunks, axis=0)
    normed = rms_norm(all_tokens.astype(F32), gains[0]).astype(BF16)
    normed = after(normed, *dy_chunks[-4:])
    qk = dot_plain(normed, w_three[:, : 2 * wide])
    v = dot_plain(normed, w_three[:, 2 * wide :]).astype(BF16)
    q, k, v, mass, mixed = attend_forward(source, first, qk, v, cosine, sine, doc_col, doc_row)

    def partial_hidden(start, stop):
        return dot_plain(chunk_rows(mixed, start, stop), out_w).astype(BF16)

    hidden = flat + scatter_rows(partial_hidden)

    second16 = rms_norm(hidden, gains[1]).astype(BF16)
    masses = lax.all_to_all(after(mass, second16).reshape(group, local), "kv", 0, 0)
    peak = jnp.max(jnp.sum(masses, axis=0)).reshape(1, 1)
    everyone = jnp.broadcast_to(peak, (ring * group, 1))
    summary = jnp.max(lax.all_to_all(everyone, ("seq", "kv"), 0, 0)).reshape(1)
    second_all = after(gather_rows(second16), summary)
    gate = dot_plain(second_all, gate_w)
    up = dot_plain(second_all, up_w)
    sig = jax.nn.sigmoid(gate)
    inner = (gate * sig * up).astype(BF16)
    grad_down = dot_left(dy_all, inner).astype(BF16)
    grads_down = lax.psum_scatter(grad_down, "seq", scatter_dimension=0, tiled=True)
    dinner = dot_right(after(dy_all, grad_down), down_w)
    dgate = (dinner * up * (sig * (1.0 + gate * (1.0 - sig)))).astype(BF16)
    dup = (dinner * (gate * sig)).astype(BF16)
    partials = []

    def partial_second(start, stop):
        partials.append(
            (
                dot_right(chunk_rows(dgate, start, stop), gate_w)
                + dot_right(chunk_rows(dup, start, stop), up_w)
            ).astype(BF16)
        )
        return partials[-1]

    grad_second = scatter_rows(partial_second)
    second_later = after(second_all, *partials)
    grads_gate = lax.psum_scatter(
        dot_left(second_later, dgate).astype(BF16), "seq", scatter_dimension=0, tiled=True
    )
    grads_up = lax.psum_scatter(
        dot_left(second_later, dup).astype(BF16), "seq", scatter_dimension=0, tiled=True
    )

    grad_hidden = dy16.astype(F32) + rms_back(hidden, gains[1], grad_second)
    dh_chunks = gather_chunks(after(grad_hidden.astype(BF16), grads_down))
    grads_down = grads_down.astype(F32).T
    dh_all = jnp.concatenate(dh_chunks, axis=0)

    def partial_result(start, stop):
        product = dot_plain(after(chunk_rows(inner, start, stop), *partials), down_w)
        return after(product.astype(BF16), *dh_chunks[-2:])

    result = hidden + scatter_rows(partial_result)
    dmixed = dot_right(dh_all, out_w).astype(BF16)
    grad_w_out = dot_left(mixed, dh_all).astype(BF16)
    dqkv = attend_backward(source, last, q, k, v, dmixed, cosine, sine, doc_col, doc_row)

    def partial_normed(start, stop):
        return dot_right(chunk_rows(dqkv, start, stop), w_three).astype(BF16)

    grad_normed = scatter_rows(partial_normed)
    grad_input = grad_hidden + rms_back(flat, gains[0], grad_normed)
    grads_gate, grads_up = after((grads_gate, grads_up), grad_input, result)

    grad_w_out = grad_w_out.reshape(mine, share, piece, width).transpose(1, 0, 2, 3)
    grad_w_out = lax.all_to_all(grad_w_out, "kv", 0, 0, axis_index_groups=pairs)
    grad_w_out = grad_w_out.reshape(ring * group * piece, width // group)
    grad_four = jnp.concatenate([dot_left(normed, dqkv).astype(BF16), grad_w_out], axis=1)
    grad_four = lax.psum_scatter(grad_four, "seq", scatter_dimension=0, tiled=True)
    grad_w_out = grad_four[:, 3 * wide :].reshape(piece, width).astype(F32)
    grad_three = grad_four[:, : 3 * wide]
    grad_three = lax.all_to_all(grad_three.reshape(group, piece, 3 * wide), "kv", 0, 0)
    grad_three = grad_three.reshape(planes, share, piece, 3, mine, HEAD_DIM)
    grad_three = grad_three.transpose(3, 2, 1, 4, 0, 5).reshape(3, piece, width).astype(F32)

    scales = jnp.stack([gain_rows(flat, grad_normed), gain_rows(hidden, grad_second)], axis=1)
    scales = lax.all_to_all(scales.reshape(ring * group, piece, 2), ("seq", "kv"), 0, 0)
    scales = jnp.sum(scales, axis=0)

    return (
        result.reshape(seqs, local, width).astype(BF16),
        grad_input.reshape(seqs, local, width),
        grad_three[0],
        grad_three[1],
        grad_three[2],
        grad_w_out,
        scales[:, 0],
        scales[:, 1],
        grads_gate.astype(F32),
        grads_up.astype(F32),
        grads_down,
        summary,
    )


def solution(mesh):
    tokens = P("seq", "kv", None)
    rows = P(("seq", "kv"), None)
    vector = P(("seq", "kv"))
    grid = P("seq", "kv")
    in_specs = (
        tokens, P("seq", "kv"), rows, rows, rows, rows, vector, vector, grid, grid,
        P("kv", "seq"), tokens,
    )
    out_specs = (
        tokens, tokens, rows, rows, rows, rows, vector, vector, grid, grid, P("kv", "seq"), P(),
    )
    return jax.shard_map(
        per_device, mesh=mesh, in_specs=in_specs, out_specs=out_specs, check_vma=False
    )
```

```python
import functools
import math

import jax
import jax.numpy as jnp
from jax import lax
from jax.experimental import pallas as pl
from jax.experimental.pallas import tpu as pltpu
from jax.sharding import PartitionSpec as P

HEAD_DIM = 128
EPSILON = 1e-05
BLOCK = 256
LOG2E = math.log2(math.e)
BF16 = jnp.bfloat16
F32 = jnp.float32


def dot_plain(left, right):
    return jnp.dot(left, right, preferred_element_type=F32)


def dot_left(left, right):
    return lax.dot_general(left, right, (((0,), (0,)), ((), ())), preferred_element_type=F32)


def dot_right(left, right):
    return lax.dot_general(left, right, (((1,), (1,)), ((), ())), preferred_element_type=F32)


def rms_norm(values, gain):
    return values * lax.rsqrt(jnp.mean(values * values, axis=-1, keepdims=True) + EPSILON) * gain


def rms_back(values, gain, grad):
    inverse = lax.rsqrt(jnp.mean(values * values, axis=-1, keepdims=True) + EPSILON)
    scaled = grad * gain
    moment = jnp.mean(values * scaled, axis=-1, keepdims=True)
    return inverse * scaled - values * (inverse * inverse * inverse) * moment


def gain_rows(values, grad):
    inverse = lax.rsqrt(jnp.mean(values * values, axis=-1, keepdims=True) + EPSILON)
    return jnp.sum(grad * values * inverse, axis=0)


ORDER = (0, 2, 4, 6, 1, 3, 5, 7)


def swap(values, mask):
    size = lax.axis_size("kv")
    return lax.ppermute(values, "kv", [(i, i ^ mask) for i in range(size)])


def owners():
    size = lax.axis_size("kv")
    if size == 8:
        return lax.axis_index("kv").astype(jnp.int32) ^ jnp.array(ORDER, jnp.int32)
    return jnp.arange(size, dtype=jnp.int32)


def gather_chunks(values):
    size = lax.axis_size("kv")
    if size != 8:
        return [lax.all_gather(values, "kv", axis=0, tiled=True)]
    half = values.shape[0] // 2
    near_x = swap(values, 2)
    near_y = swap(values, 4)
    core = swap(values, 1)
    far_top = swap(near_x[:half], 4)
    far_low = swap(near_y[half:], 2)
    core_x = swap(near_x, 1)
    core_y = swap(near_y, 1)
    core_top = swap(far_top, 1)
    core_low = swap(far_low, 1)
    return [values, near_x, near_y, far_top, far_low, core, core_x, core_y, core_top, core_low]


def gather_rows(values):
    return jnp.concatenate(gather_chunks(values), axis=0)


def add16(left, right):
    return (left.astype(F32) + right.astype(F32)).astype(BF16)


def scatter_rows(make, seen):
    size = lax.axis_size("kv")
    if size != 8:
        full = make(0, size)
        seen.append(full)
        return lax.psum_scatter(full, "kv", scatter_dimension=0, tiled=True).astype(F32)
    odd = make(4, 8)
    theirs = swap(odd, 1)
    even = make(0, 4)
    local = even.shape[0] // 4
    half = local // 2

    def both(chunk, low):
        rows = slice(chunk * local + low * half, chunk * local + (low + 1) * half)
        return add16(even[rows], theirs[rows])

    send_x, send_y = lax.optimization_barrier(
        (
            jnp.concatenate([both(1, 0), both(3, 0)], axis=0),
            jnp.concatenate([both(2, 1), both(3, 1)], axis=0),
        )
    )
    from_x, from_y = lax.optimization_barrier((swap(send_x, 2), swap(send_y, 4)))
    send_y, send_x = lax.optimization_barrier(
        (add16(both(2, 0), from_x[half:]), add16(both(1, 1), from_y[half:]))
    )
    last_y, last_x = lax.optimization_barrier((swap(send_y, 4), swap(send_x, 2)))
    seen += [last_y, last_x]
    top = both(0, 0).astype(F32) + from_x[:half].astype(F32) + last_y.astype(F32)
    low = both(0, 1).astype(F32) + from_y[:half].astype(F32) + last_x.astype(F32)
    return jnp.concatenate([top, low], axis=0)


def after(values, *others):
    return lax.optimization_barrier((values,) + tuple(others))[0]


def spread_small(values, axis):
    size = lax.axis_size(axis)
    return lax.all_to_all(jnp.broadcast_to(values[None], (size,) + values.shape), axis, 0, 0)


def turn(values, cosine, sine):
    return values * cosine + pltpu.roll(values, HEAD_DIM // 2, 1) * sine


def forward_kernel(
    heads, parts, length, scale, offset,
    source, first, qk_hbm, v_hbm, cos_ref, sin_ref, doc_col, doc_row,
    q_ref, k_ref, v_ref, mass_ref, mixed_hbm,
    qk_s, mixed_s, sems,
):
    wide = heads * HEAD_DIM
    rows = length // parts

    def load(b):
        start = pl.multiple_of(source[b] * rows, rows)
        here = pl.ds(b * rows, rows)
        return (
            pltpu.make_async_copy(qk_hbm.at[pl.ds(start, rows), :], qk_s.at[here, :], sems.at[0, b]),
            pltpu.make_async_copy(v_hbm.at[pl.ds(start, rows), :], v_ref.at[here, :], sems.at[1, b]),
        )

    def store(b):
        start = pl.multiple_of(source[b] * rows, rows)
        return pltpu.make_async_copy(
            mixed_s.at[pl.ds(b * rows, rows), :], mixed_hbm.at[pl.ds(start, rows), :], sems.at[2, b]
        )

    for b in range(parts):
        for copy in load(b):
            copy.start()
    for b in range(parts):
        for copy in load(b):
            copy.wait()

    def rope(b, carry):
        here = pl.ds(pl.multiple_of(b * BLOCK, BLOCK), BLOCK)
        cosine = cos_ref[here, :]
        sine = sin_ref[here, :]
        for h in range(heads):
            lanes = slice(h * HEAD_DIM, (h + 1) * HEAD_DIM)
            more = slice(wide + h * HEAD_DIM, wide + (h + 1) * HEAD_DIM)
            q_ref[here, lanes] = turn(qk_s[here, lanes], cosine, sine).astype(BF16)
            k_ref[here, lanes] = turn(qk_s[here, more], cosine, sine).astype(BF16)
        return carry

    lax.fori_loop(0, length // BLOCK, rope, 0)

    def query_block(i, carry):
        here = pl.ds(pl.multiple_of(i * BLOCK, BLOCK), BLOCK)
        docs = doc_col[here, :]
        row = lax.broadcasted_iota(jnp.int32, (BLOCK, BLOCK), 0)
        col = lax.broadcasted_iota(jnp.int32, (BLOCK, BLOCK), 1)

        def key_block(j, carry):
            accs, mass = carry
            there = pl.ds(pl.multiple_of(j * BLOCK, BLOCK), BLOCK)
            allowed = (docs == doc_row[:, there]) & (row + (i - j) * BLOCK >= col)
            out = []
            for h in range(heads):
                lanes = slice(h * HEAD_DIM, (h + 1) * HEAD_DIM)
                score = dot_right(q_ref[here, lanes], k_ref[there, lanes])
                prob = 1.0 / (1.0 + jnp.exp2(score * (-scale * LOG2E) + offset * LOG2E))
                prob = jnp.where(allowed, prob, 0.0)
                for part in range(BLOCK // 128):
                    mass = mass + prob[:, part * 128 : (part + 1) * 128]
                out.append(accs[h] + dot_plain(prob.astype(BF16), v_ref[there, lanes]))
            return (tuple(out), mass)

        zero = jnp.zeros((BLOCK, HEAD_DIM), F32)
        accs, mass = lax.fori_loop(first[i], i + 1, key_block, ((zero,) * heads, zero))
        for h in range(heads):
            mixed_s[here, h * HEAD_DIM : (h + 1) * HEAD_DIM] = accs[h].astype(BF16)
        mass_ref[here, :] = jnp.sum(mass, axis=1, keepdims=True)
        return carry

    lax.fori_loop(0, length // BLOCK, query_block, 0)
    for b in range(parts):
        store(b).start()
    for b in range(parts):
        store(b).wait()


def attend_forward(source, first, qk, v, cosine, sine, doc_col, doc_row):
    length, wide = v.shape
    heads = wide // HEAD_DIM
    parts = source.shape[0]
    vmem = pl.BlockSpec(memory_space=pltpu.VMEM)
    smem = pl.BlockSpec(memory_space=pltpu.SMEM)
    hbm = pl.BlockSpec(memory_space=pl.ANY)
    same = jax.ShapeDtypeStruct((length, wide), BF16)
    return pl.pallas_call(
        functools.partial(
            forward_kernel, heads, parts, length, 1.0 / math.sqrt(HEAD_DIM), math.log(length)
        ),
        name="attend_forward",
        out_shape=(same, same, same, jax.ShapeDtypeStruct((length, 1), F32), same),
        in_specs=[smem, smem, hbm, hbm, vmem, vmem, vmem, vmem],
        out_specs=(vmem, vmem, vmem, vmem, hbm),
        scratch_shapes=[
            pltpu.VMEM((length, 2 * wide), F32),
            pltpu.VMEM((length, wide), BF16),
            pltpu.SemaphoreType.DMA((3, parts)),
        ],
        cost_estimate=pl.CostEstimate(
            flops=2 * length * length * wide,
            transcendentals=length * length * heads,
            bytes_accessed=length * wide * 18,
        ),
    )(source, first, qk, v, cosine, sine, doc_col, doc_row)


def backward_kernel(
    heads, parts, length, scale, offset,
    source, last, q_ref, k_ref, v_ref, g_hbm, cos_ref, sin_ref, doc_col, doc_row,
    out_hbm,
    g_s, dq_s, out_s, sems,
):
    wide = heads * HEAD_DIM
    rows = length // parts

    def load(b):
        start = pl.multiple_of(source[b] * rows, rows)
        return pltpu.make_async_copy(
            g_hbm.at[pl.ds(start, rows), :], g_s.at[pl.ds(b * rows, rows), :], sems.at[0, b]
        )

    def store(b):
        start = pl.multiple_of(source[b] * rows, rows)
        return pltpu.make_async_copy(
            out_s.at[pl.ds(b * rows, rows), :], out_hbm.at[pl.ds(start, rows), :], sems.at[1, b]
        )

    for b in range(parts):
        load(b).start()
    dq_s[...] = jnp.zeros_like(dq_s)
    for b in range(parts):
        load(b).wait()

    def key_block(j, carry):
        there = pl.ds(pl.multiple_of(j * BLOCK, BLOCK), BLOCK)
        docs = doc_col[there, :]
        row = lax.broadcasted_iota(jnp.int32, (BLOCK, BLOCK), 0)
        col = lax.broadcasted_iota(jnp.int32, (BLOCK, BLOCK), 1)

        def query_block(i, carry):
            dks, dvs = carry
            here = pl.ds(pl.multiple_of(i * BLOCK, BLOCK), BLOCK)
            allowed = (docs == doc_row[:, here]) & (col + (i - j) * BLOCK >= row)
            new_k, new_v = [], []
            for h in range(heads):
                lanes = slice(h * HEAD_DIM, (h + 1) * HEAD_DIM)
                query = q_ref[here, lanes]
                grad = g_s[here, lanes]
                score = dot_right(k_ref[there, lanes], query)
                prob = 1.0 / (1.0 + jnp.exp2(score * (-scale * LOG2E) + offset * LOG2E))
                prob = jnp.where(allowed, prob, 0.0)
                new_v.append(dvs[h] + dot_plain(prob.astype(BF16), grad))
                dprob = dot_right(v_ref[there, lanes], grad)
                dscore = (dprob * (prob - prob * prob)).astype(BF16)
                new_k.append(dks[h] + dot_plain(dscore, query))
                dq_s[here, lanes] += dot_left(dscore, k_ref[there, lanes])
            return (tuple(new_k), tuple(new_v))

        zero = (jnp.zeros((BLOCK, HEAD_DIM), F32),) * heads
        dks, dvs = lax.fori_loop(j, last[j], query_block, (zero, zero))
        cosine = cos_ref[there, :]
        sine = sin_ref[there, :]
        for h in range(heads):
            lanes = slice(h * HEAD_DIM, (h + 1) * HEAD_DIM)
            more = slice(wide + h * HEAD_DIM, wide + (h + 1) * HEAD_DIM)
            most = slice(2 * wide + h * HEAD_DIM, 2 * wide + (h + 1) * HEAD_DIM)
            out_s[there, lanes] = turn(dq_s[there, lanes] * scale, cosine, -sine).astype(BF16)
            out_s[there, more] = turn(dks[h] * scale, cosine, -sine).astype(BF16)
            out_s[there, most] = dvs[h].astype(BF16)
        return carry

    lax.fori_loop(0, length // BLOCK, key_block, 0)
    for b in range(parts):
        store(b).start()
    for b in range(parts):
        store(b).wait()


def attend_backward(source, last, q, k, v, grad, cosine, sine, doc_col, doc_row):
    length, wide = v.shape
    heads = wide // HEAD_DIM
    parts = source.shape[0]
    vmem = pl.BlockSpec(memory_space=pltpu.VMEM)
    smem = pl.BlockSpec(memory_space=pltpu.SMEM)
    hbm = pl.BlockSpec(memory_space=pl.ANY)
    return pl.pallas_call(
        functools.partial(
            backward_kernel, heads, parts, length, 1.0 / math.sqrt(HEAD_DIM), math.log(length)
        ),
        name="attend_backward",
        out_shape=jax.ShapeDtypeStruct((length, 3 * wide), BF16),
        in_specs=[smem, smem, vmem, vmem, vmem, hbm, vmem, vmem, vmem, vmem],
        out_specs=hbm,
        scratch_shapes=[
            pltpu.VMEM((length, wide), BF16),
            pltpu.VMEM((length, wide), F32),
            pltpu.VMEM((length, 3 * wide), BF16),
            pltpu.SemaphoreType.DMA((2, parts)),
        ],
        cost_estimate=pl.CostEstimate(
            flops=5 * length * length * wide,
            transcendentals=length * length * heads,
            bytes_accessed=length * wide * 14,
        ),
    )(source, last, q, k, v, grad, cosine, sine, doc_col, doc_row)


def per_device(
    tokens,
    doc_ids,
    w_query,
    w_key,
    w_value,
    w_out,
    gain_attn,
    gain_ffn,
    w_gate,
    w_up,
    w_down,
    cotangent,
):
    ring = lax.axis_size("seq")
    group = lax.axis_size("kv")
    seqs, local, width = tokens.shape
    length = local * group
    piece = w_query.shape[0]
    heads = width // HEAD_DIM
    planes = heads // ring
    share = group // planes
    mine = ring // share
    wide = mine * HEAD_DIM
    pairs = [[j * share + c for c in range(share)] for j in range(planes)]

    def chunk_rows(values, start, stop):
        return values[start * local : stop * local]

    flat16 = tokens.reshape(local, width)
    flat = flat16.astype(F32)
    dy16 = cotangent.reshape(local, width)

    w_three = jnp.stack([w_query, w_key, w_value])
    w_three = w_three.reshape(3, piece, share, mine, planes, HEAD_DIM)
    w_three = w_three.transpose(4, 2, 1, 0, 3, 5).reshape(group, piece, 3 * wide)
    w_three = lax.all_to_all(w_three, "kv", 0, 0).reshape(group * piece, 3 * wide)
    w_three = lax.all_gather(w_three, "seq", axis=0, tiled=True)
    out_w = lax.all_gather(w_out, "seq", axis=0, tiled=False)
    out_w = lax.all_to_all(
        out_w.reshape(share, mine, piece, width), "kv", 0, 0, axis_index_groups=pairs
    )
    out_w = out_w.transpose(1, 0, 2, 3).reshape(wide, width)
    gate_w = lax.all_gather(w_gate, "seq", axis=0, tiled=True)
    up_w = lax.all_gather(w_up, "seq", axis=0, tiled=True)
    down_w = lax.all_gather(w_down, "seq", axis=1, tiled=True)

    gains = spread_small(spread_small(jnp.stack([gain_attn, gain_ffn]), "kv"), "seq")
    gains = gains.transpose(2, 0, 1, 3).reshape(2, width).astype(F32)
    ids = spread_small(doc_ids.reshape(local), "kv")

    half = local // 2
    by_pos = jnp.concatenate([ids[:, :half], ids[::-1, half:]], axis=0).reshape(length)
    blocks = length // BLOCK
    starts = by_pos.reshape(blocks, BLOCK)[:, 0]
    ends = by_pos.reshape(blocks, BLOCK)[:, -1]
    first = jnp.sum((by_pos[None] < starts[:, None]).astype(jnp.int32), axis=1) // BLOCK
    last = (jnp.sum((by_pos[None] <= ends[:, None]).astype(jnp.int32), axis=1) + BLOCK - 1) // BLOCK
    doc_col = by_pos.reshape(length, 1)
    doc_row = by_pos.reshape(1, length)
    order = jnp.argsort(owners()).astype(jnp.int32) if group != 8 else None
    if group == 8:
        where = [ORDER.index(m) for m in range(8)]
        order = jnp.array(where, jnp.int32)[
            lax.axis_index("kv").astype(jnp.int32) ^ jnp.arange(8, dtype=jnp.int32)
        ]
    source = jnp.concatenate([2 * order, 2 * order[::-1] + 1])

    angle = jnp.arange(length, dtype=F32)[:, None] * jnp.exp(
        jnp.arange(HEAD_DIM // 2, dtype=F32) * (-2.0 * math.log(10000.0) / HEAD_DIM)
    )
    cosine = jnp.cos(angle)
    sine = jnp.sin(angle)
    cosine = jnp.concatenate([cosine, cosine], axis=1)
    sine = jnp.concatenate([-sine, sine], axis=1)

    token_chunks = gather_chunks(flat16)
    all_tokens = jnp.concatenate(token_chunks, axis=0)
    dy_chunks = gather_chunks(after(dy16, *token_chunks[-2:]))
    dy_all = jnp.concatenate(dy_chunks, axis=0)
    normed = rms_norm(all_tokens.astype(F32), gains[0]).astype(BF16)
    normed = after(normed, *dy_chunks[-4:])
    qk = dot_plain(normed, w_three[:, : 2 * wide])
    v = dot_plain(normed, w_three[:, 2 * wide :]).astype(BF16)
    q, k, v, mass, mixed = attend_forward(source, first, qk, v, cosine, sine, doc_col, doc_row)

    def partial_hidden(start, stop):
        return dot_plain(chunk_rows(mixed, start, stop), out_w).astype(BF16)

    hidden = flat + scatter_rows(partial_hidden, [])

    second16 = rms_norm(hidden, gains[1]).astype(BF16)
    masses = lax.all_to_all(after(mass, second16).reshape(group, local), "kv", 0, 0)
    peak = jnp.max(jnp.sum(masses, axis=0)).reshape(1, 1)
    everyone = jnp.broadcast_to(peak, (ring * group, 1))
    summary = jnp.max(lax.all_to_all(everyone, ("seq", "kv"), 0, 0)).reshape(1)
    second_all = after(gather_rows(second16), summary)
    gate = dot_plain(second_all, gate_w)
    up = dot_plain(second_all, up_w)
    sig = jax.nn.sigmoid(gate)
    inner = (gate * sig * up).astype(BF16)
    grad_down = dot_left(dy_all, inner).astype(BF16)
    grads_down = lax.psum_scatter(grad_down, "seq", scatter_dimension=0, tiled=True)
    dinner = dot_right(after(dy_all, grad_down), down_w)
    dgate = (dinner * up * (sig * (1.0 + gate * (1.0 - sig)))).astype(BF16)
    dup = (dinner * (gate * sig)).astype(BF16)
    partials = []

    def partial_second(start, stop):
        partials.append(
            (
                dot_right(chunk_rows(dgate, start, stop), gate_w)
                + dot_right(chunk_rows(dup, start, stop), up_w)
            ).astype(BF16)
        )
        return partials[-1]

    grad_second = scatter_rows(partial_second, [])
    grads_gate = lax.psum_scatter(
        dot_left(after(second_all, *partials), dgate).astype(BF16), "seq", scatter_dimension=0, tiled=True
    )
    grad_hidden = dy16.astype(F32) + rms_back(hidden, gains[1], grad_second)
    dh_chunks = gather_chunks(after(grad_hidden.astype(BF16), grads_down))
    grads_down = grads_down.astype(F32).T
    dh_all = jnp.concatenate(dh_chunks, axis=0)

    def partial_result(start, stop):
        product = dot_plain(after(chunk_rows(inner, start, stop), *partials), down_w)
        return after(product.astype(BF16), *dh_chunks[-2:])

    ends, normed_parts = [], []
    result = hidden + scatter_rows(partial_result, ends)
    dmixed = dot_right(dh_all, out_w).astype(BF16)
    grad_w_out = dot_left(mixed, dh_all).astype(BF16)
    dqkv = attend_backward(source, last, q, k, v, dmixed, cosine, sine, doc_col, doc_row)

    def partial_normed(start, stop):
        product = dot_right(after(chunk_rows(dqkv, start, stop), grads_gate), w_three)
        normed_parts.append(product.astype(BF16))
        return normed_parts[-1]

    grad_normed = scatter_rows(partial_normed, ends)
    grad_input = grad_hidden + rms_back(flat, gains[0], grad_normed)

    grad_w_out = grad_w_out.reshape(mine, share, piece, width).transpose(1, 0, 2, 3)
    grad_w_out = lax.all_to_all(grad_w_out, "kv", 0, 0, axis_index_groups=pairs)
    grad_w_out = grad_w_out.reshape(ring * group * piece, width // group)
    grad_four = jnp.concatenate([dot_left(normed, dqkv).astype(BF16), grad_w_out], axis=1)
    grad_four = lax.psum_scatter(grad_four, "seq", scatter_dimension=0, tiled=True)
    grads_up = lax.psum_scatter(
        dot_left(after(second_all, *normed_parts), dup).astype(BF16),
        "seq", scatter_dimension=0, tiled=True,
    )
    grad_w_out = grad_four[:, 3 * wide :].reshape(piece, width).astype(F32)
    grad_three = grad_four[:, : 3 * wide]
    grad_three = lax.all_to_all(grad_three.reshape(group, piece, 3 * wide), "kv", 0, 0)
    grads_up = after(grads_up, grad_three, *ends)
    grad_three = grad_three.reshape(planes, share, piece, 3, mine, HEAD_DIM)
    grad_three = grad_three.transpose(3, 2, 1, 4, 0, 5).reshape(3, piece, width).astype(F32)

    scales = jnp.stack([gain_rows(flat, grad_normed), gain_rows(hidden, grad_second)], axis=1)
    scales = lax.all_to_all(scales.reshape(ring * group, piece, 2), ("seq", "kv"), 0, 0)
    scales = jnp.sum(scales, axis=0)

    return (
        result.reshape(seqs, local, width).astype(BF16),
        grad_input.reshape(seqs, local, width),
        grad_three[0],
        grad_three[1],
        grad_three[2],
        grad_w_out,
        scales[:, 0],
        scales[:, 1],
        grads_gate.astype(F32),
        grads_up.astype(F32),
        grads_down,
        summary,
    )


def solution(mesh):
    tokens = P("seq", "kv", None)
    rows = P(("seq", "kv"), None)
    vector = P(("seq", "kv"))
    grid = P("seq", "kv")
    in_specs = (
        tokens, P("seq", "kv"), rows, rows, rows, rows, vector, vector, grid, grid,
        P("kv", "seq"), tokens,
    )
    out_specs = (
        tokens, tokens, rows, rows, rows, rows, vector, vector, grid, grid, P("kv", "seq"), P(),
    )
    return jax.shard_map(
        per_device, mesh=mesh, in_specs=in_specs, out_specs=out_specs, check_vma=False
    )
```

```python
import functools
import math

import jax
import jax.numpy as jnp
from jax import lax
from jax.experimental import pallas as pl
from jax.experimental.layout import Layout, with_layout_constraint
from jax.experimental.pallas import tpu as pltpu
from jax.sharding import PartitionSpec as P

HEAD_DIM = 128
EPSILON = 1e-05
BLOCK = 256
LOG2E = math.log2(math.e)
BF16 = jnp.bfloat16
F32 = jnp.float32


def dot_plain(left, right):
    return jnp.dot(left, right, preferred_element_type=F32)


def dot_left(left, right):
    return lax.dot_general(left, right, (((0,), (0,)), ((), ())), preferred_element_type=F32)


def dot_right(left, right):
    return lax.dot_general(left, right, (((1,), (1,)), ((), ())), preferred_element_type=F32)


def rms_norm(values, gain):
    return values * lax.rsqrt(jnp.mean(values * values, axis=-1, keepdims=True) + EPSILON) * gain


def rms_back(values, gain, grad):
    inverse = lax.rsqrt(jnp.mean(values * values, axis=-1, keepdims=True) + EPSILON)
    scaled = grad * gain
    moment = jnp.mean(values * scaled, axis=-1, keepdims=True)
    return inverse * scaled - values * (inverse * inverse * inverse) * moment


def gain_rows(values, grad):
    inverse = lax.rsqrt(jnp.mean(values * values, axis=-1, keepdims=True) + EPSILON)
    return jnp.sum(grad * values * inverse, axis=0)


ORDER = (0, 2, 4, 6, 1, 3, 5, 7)


def swap(values, mask):
    size = lax.axis_size("kv")
    return lax.ppermute(values, "kv", [(i, i ^ mask) for i in range(size)])


def owners():
    size = lax.axis_size("kv")
    if size == 8:
        return lax.axis_index("kv").astype(jnp.int32) ^ jnp.array(ORDER, jnp.int32)
    return jnp.arange(size, dtype=jnp.int32)


def gather_chunks(values):
    size = lax.axis_size("kv")
    if size != 8:
        return [lax.all_gather(values, "kv", axis=0, tiled=True)]
    half = values.shape[0] // 2
    near_x = swap(values, 2)
    near_y = swap(values, 4)
    core = swap(values, 1)
    far_top = swap(near_x[:half], 4)
    far_low = swap(near_y[half:], 2)
    core_x = swap(near_x, 1)
    core_y = swap(near_y, 1)
    core_top = swap(far_top, 1)
    core_low = swap(far_low, 1)
    return [values, near_x, near_y, far_top, far_low, core, core_x, core_y, core_top, core_low]


def gather_rows(values):
    return jnp.concatenate(gather_chunks(values), axis=0)


def add16(left, right):
    return (left.astype(F32) + right.astype(F32)).astype(BF16)


def scatter_rows(make, seen):
    size = lax.axis_size("kv")
    if size != 8:
        full = make(0, size)
        seen.append(full)
        return lax.psum_scatter(full, "kv", scatter_dimension=0, tiled=True).astype(F32)
    odd = make(4, 8)
    theirs = swap(odd, 1)
    even = make(0, 4)
    local = even.shape[0] // 4
    half = local // 2

    def both(chunk, low):
        rows = slice(chunk * local + low * half, chunk * local + (low + 1) * half)
        return add16(even[rows], theirs[rows])

    send_x, send_y = lax.optimization_barrier(
        (
            jnp.concatenate([both(1, 0), both(3, 0)], axis=0),
            jnp.concatenate([both(2, 1), both(3, 1)], axis=0),
        )
    )
    from_x, from_y = lax.optimization_barrier((swap(send_x, 2), swap(send_y, 4)))
    send_y, send_x = lax.optimization_barrier(
        (add16(both(2, 0), from_x[half:]), add16(both(1, 1), from_y[half:]))
    )
    last_y, last_x = lax.optimization_barrier((swap(send_y, 4), swap(send_x, 2)))
    seen += [last_y, last_x]
    top = both(0, 0).astype(F32) + from_x[:half].astype(F32) + last_y.astype(F32)
    low = both(0, 1).astype(F32) + from_y[:half].astype(F32) + last_x.astype(F32)
    return jnp.concatenate([top, low], axis=0)


def after(values, *others):
    return lax.optimization_barrier((values,) + tuple(others))[0]


def spread_small(values, axis):
    size = lax.axis_size(axis)
    return lax.all_to_all(jnp.broadcast_to(values[None], (size,) + values.shape), axis, 0, 0)


def turn(values, cosine, sine):
    return values * cosine + pltpu.roll(values, HEAD_DIM // 2, 1) * sine


def forward_kernel(
    heads, parts, length, scale, offset,
    source, first, qk_hbm, v_hbm, cos_ref, sin_ref, doc_col, doc_row,
    q_ref, k_ref, v_ref, mass_ref, mixed_hbm,
    qk_s, mixed_s, sems,
):
    wide = heads * HEAD_DIM
    rows = length // parts

    def load(b):
        start = pl.multiple_of(source[b] * rows, rows)
        here = pl.ds(b * rows, rows)
        return (
            pltpu.make_async_copy(qk_hbm.at[pl.ds(start, rows), :], qk_s.at[here, :], sems.at[0, b]),
            pltpu.make_async_copy(v_hbm.at[pl.ds(start, rows), :], v_ref.at[here, :], sems.at[1, b]),
        )

    def store(b):
        start = pl.multiple_of(source[b] * rows, rows)
        return pltpu.make_async_copy(
            mixed_s.at[pl.ds(b * rows, rows), :], mixed_hbm.at[pl.ds(start, rows), :], sems.at[2, b]
        )

    for b in range(parts):
        for copy in load(b):
            copy.start()
    for b in range(parts):
        for copy in load(b):
            copy.wait()

    def rope(b, carry):
        here = pl.ds(pl.multiple_of(b * BLOCK, BLOCK), BLOCK)
        cosine = cos_ref[here, :]
        sine = sin_ref[here, :]
        for h in range(heads):
            lanes = slice(h * HEAD_DIM, (h + 1) * HEAD_DIM)
            more = slice(wide + h * HEAD_DIM, wide + (h + 1) * HEAD_DIM)
            q_ref[here, lanes] = turn(qk_s[here, lanes], cosine, sine).astype(BF16)
            k_ref[here, lanes] = turn(qk_s[here, more], cosine, sine).astype(BF16)
        return carry

    lax.fori_loop(0, length // BLOCK, rope, 0)

    def query_block(i, carry):
        here = pl.ds(pl.multiple_of(i * BLOCK, BLOCK), BLOCK)
        docs = doc_col[here, :]
        row = lax.broadcasted_iota(jnp.int32, (BLOCK, BLOCK), 0)
        col = lax.broadcasted_iota(jnp.int32, (BLOCK, BLOCK), 1)

        def key_block(j, carry):
            accs, mass = carry
            there = pl.ds(pl.multiple_of(j * BLOCK, BLOCK), BLOCK)
            allowed = (docs == doc_row[:, there]) & (row + (i - j) * BLOCK >= col)
            out = []
            for h in range(heads):
                lanes = slice(h * HEAD_DIM, (h + 1) * HEAD_DIM)
                score = dot_right(q_ref[here, lanes], k_ref[there, lanes])
                prob = 1.0 / (1.0 + jnp.exp2(score * (-scale * LOG2E) + offset * LOG2E))
                prob = jnp.where(allowed, prob, 0.0)
                for part in range(BLOCK // 128):
                    mass = mass + prob[:, part * 128 : (part + 1) * 128]
                out.append(accs[h] + dot_plain(prob.astype(BF16), v_ref[there, lanes]))
            return (tuple(out), mass)

        zero = jnp.zeros((BLOCK, HEAD_DIM), F32)
        accs, mass = lax.fori_loop(first[i], i + 1, key_block, ((zero,) * heads, zero))
        for h in range(heads):
            mixed_s[here, h * HEAD_DIM : (h + 1) * HEAD_DIM] = accs[h].astype(BF16)
        mass_ref[here, :] = jnp.sum(mass, axis=1, keepdims=True)
        return carry

    lax.fori_loop(0, length // BLOCK, query_block, 0)
    for b in range(parts):
        store(b).start()
    for b in range(parts):
        store(b).wait()


def attend_forward(source, first, qk, v, cosine, sine, doc_col, doc_row):
    length, wide = v.shape
    heads = wide // HEAD_DIM
    parts = source.shape[0]
    vmem = pl.BlockSpec(memory_space=pltpu.VMEM)
    smem = pl.BlockSpec(memory_space=pltpu.SMEM)
    hbm = pl.BlockSpec(memory_space=pl.ANY)
    same = jax.ShapeDtypeStruct((length, wide), BF16)
    return pl.pallas_call(
        functools.partial(
            forward_kernel, heads, parts, length, 1.0 / math.sqrt(HEAD_DIM), math.log(length)
        ),
        name="attend_forward",
        out_shape=(same, same, same, jax.ShapeDtypeStruct((length, 1), F32), same),
        in_specs=[smem, smem, hbm, hbm, vmem, vmem, vmem, vmem],
        out_specs=(vmem, vmem, vmem, vmem, hbm),
        scratch_shapes=[
            pltpu.VMEM((length, 2 * wide), F32),
            pltpu.VMEM((length, wide), BF16),
            pltpu.SemaphoreType.DMA((3, parts)),
        ],
        cost_estimate=pl.CostEstimate(
            flops=2 * length * length * wide,
            transcendentals=length * length * heads,
            bytes_accessed=length * wide * 18,
        ),
    )(source, first, qk, v, cosine, sine, doc_col, doc_row)


def backward_kernel(
    heads, parts, length, scale, offset,
    source, last, q_ref, k_ref, v_ref, g_hbm, cos_ref, sin_ref, doc_col, doc_row,
    out_hbm,
    g_s, dq_s, out_s, sems,
):
    wide = heads * HEAD_DIM
    rows = length // parts

    def load(b):
        start = pl.multiple_of(source[b] * rows, rows)
        return pltpu.make_async_copy(
            g_hbm.at[pl.ds(start, rows), :], g_s.at[pl.ds(b * rows, rows), :], sems.at[0, b]
        )

    def store(b):
        start = pl.multiple_of(source[b] * rows, rows)
        return pltpu.make_async_copy(
            out_s.at[pl.ds(b * rows, rows), :], out_hbm.at[pl.ds(start, rows), :], sems.at[1, b]
        )

    for b in range(parts):
        load(b).start()
    dq_s[...] = jnp.zeros_like(dq_s)
    for b in range(parts):
        load(b).wait()

    def key_block(j, carry):
        there = pl.ds(pl.multiple_of(j * BLOCK, BLOCK), BLOCK)
        docs = doc_col[there, :]
        row = lax.broadcasted_iota(jnp.int32, (BLOCK, BLOCK), 0)
        col = lax.broadcasted_iota(jnp.int32, (BLOCK, BLOCK), 1)

        def query_block(i, carry):
            dks, dvs = carry
            here = pl.ds(pl.multiple_of(i * BLOCK, BLOCK), BLOCK)
            allowed = (docs == doc_row[:, here]) & (col + (i - j) * BLOCK >= row)
            new_k, new_v = [], []
            for h in range(heads):
                lanes = slice(h * HEAD_DIM, (h + 1) * HEAD_DIM)
                query = q_ref[here, lanes]
                grad = g_s[here, lanes]
                score = dot_right(k_ref[there, lanes], query)
                prob = 1.0 / (1.0 + jnp.exp2(score * (-scale * LOG2E) + offset * LOG2E))
                prob = jnp.where(allowed, prob, 0.0)
                new_v.append(dvs[h] + dot_plain(prob.astype(BF16), grad))
                dprob = dot_right(v_ref[there, lanes], grad)
                dscore = (dprob * (prob - prob * prob)).astype(BF16)
                new_k.append(dks[h] + dot_plain(dscore, query))
                dq_s[here, lanes] += dot_left(dscore, k_ref[there, lanes])
            return (tuple(new_k), tuple(new_v))

        zero = (jnp.zeros((BLOCK, HEAD_DIM), F32),) * heads
        dks, dvs = lax.fori_loop(j, last[j], query_block, (zero, zero))
        cosine = cos_ref[there, :]
        sine = sin_ref[there, :]
        for h in range(heads):
            lanes = slice(h * HEAD_DIM, (h + 1) * HEAD_DIM)
            more = slice(wide + h * HEAD_DIM, wide + (h + 1) * HEAD_DIM)
            most = slice(2 * wide + h * HEAD_DIM, 2 * wide + (h + 1) * HEAD_DIM)
            out_s[there, lanes] = turn(dq_s[there, lanes] * scale, cosine, -sine).astype(BF16)
            out_s[there, more] = turn(dks[h] * scale, cosine, -sine).astype(BF16)
            out_s[there, most] = dvs[h].astype(BF16)
        return carry

    lax.fori_loop(0, length // BLOCK, key_block, 0)
    for b in range(parts):
        store(b).start()
    for b in range(parts):
        store(b).wait()


def attend_backward(source, last, q, k, v, grad, cosine, sine, doc_col, doc_row):
    length, wide = v.shape
    heads = wide // HEAD_DIM
    parts = source.shape[0]
    vmem = pl.BlockSpec(memory_space=pltpu.VMEM)
    smem = pl.BlockSpec(memory_space=pltpu.SMEM)
    hbm = pl.BlockSpec(memory_space=pl.ANY)
    return pl.pallas_call(
        functools.partial(
            backward_kernel, heads, parts, length, 1.0 / math.sqrt(HEAD_DIM), math.log(length)
        ),
        name="attend_backward",
        out_shape=jax.ShapeDtypeStruct((length, 3 * wide), BF16),
        in_specs=[smem, smem, vmem, vmem, vmem, hbm, vmem, vmem, vmem, vmem],
        out_specs=hbm,
        scratch_shapes=[
            pltpu.VMEM((length, wide), BF16),
            pltpu.VMEM((length, wide), F32),
            pltpu.VMEM((length, 3 * wide), BF16),
            pltpu.SemaphoreType.DMA((2, parts)),
        ],
        cost_estimate=pl.CostEstimate(
            flops=5 * length * length * wide,
            transcendentals=length * length * heads,
            bytes_accessed=length * wide * 14,
        ),
    )(source, last, q, k, v, grad, cosine, sine, doc_col, doc_row)


def per_device(
    tokens,
    doc_ids,
    w_query,
    w_key,
    w_value,
    w_out,
    gain_attn,
    gain_ffn,
    w_gate,
    w_up,
    w_down,
    cotangent,
):
    ring = lax.axis_size("seq")
    group = lax.axis_size("kv")
    seqs, local, width = tokens.shape
    length = local * group
    piece = w_query.shape[0]
    heads = width // HEAD_DIM
    planes = heads // ring
    share = group // planes
    mine = ring // share
    wide = mine * HEAD_DIM
    pairs = [[j * share + c for c in range(share)] for j in range(planes)]

    def chunk_rows(values, start, stop):
        return values[start * local : stop * local]

    flat16 = tokens.reshape(local, width)
    flat = flat16.astype(F32)
    dy16 = cotangent.reshape(local, width)

    w_three = jnp.stack([w_query, w_key, w_value])
    w_three = w_three.reshape(3, piece, share, mine, planes, HEAD_DIM)
    w_three = w_three.transpose(4, 2, 1, 0, 3, 5).reshape(group, piece, 3 * wide)
    w_three = lax.all_to_all(w_three, "kv", 0, 0).reshape(group * piece, 3 * wide)
    w_three = lax.all_gather(w_three, "seq", axis=0, tiled=True)
    out_w = lax.all_gather(w_out, "seq", axis=0, tiled=False)
    out_w = lax.all_to_all(
        out_w.reshape(share, mine, piece, width), "kv", 0, 0, axis_index_groups=pairs
    )
    out_w = out_w.transpose(1, 0, 2, 3).reshape(wide, width)
    units = w_gate.shape[1]
    gate_up_w = jnp.concatenate([w_gate, w_up], axis=1)
    gate_up_w = lax.all_gather(gate_up_w, "seq", axis=0, tiled=True)
    gate_w, up_w = gate_up_w[:, :units], gate_up_w[:, units:]
    down_w = lax.all_gather(w_down, "seq", axis=1, tiled=True)

    gains = spread_small(spread_small(jnp.stack([gain_attn, gain_ffn]), "kv"), "seq")
    gains = gains.transpose(2, 0, 1, 3).reshape(2, width).astype(F32)
    ids = spread_small(doc_ids.reshape(local), "kv")

    half = local // 2
    by_pos = jnp.concatenate([ids[:, :half], ids[::-1, half:]], axis=0).reshape(length)
    blocks = length // BLOCK
    starts = by_pos.reshape(blocks, BLOCK)[:, 0]
    ends = by_pos.reshape(blocks, BLOCK)[:, -1]
    first = jnp.sum((by_pos[None] < starts[:, None]).astype(jnp.int32), axis=1) // BLOCK
    last = (jnp.sum((by_pos[None] <= ends[:, None]).astype(jnp.int32), axis=1) + BLOCK - 1) // BLOCK
    doc_col = by_pos.reshape(length, 1)
    doc_row = by_pos.reshape(1, length)
    order = jnp.argsort(owners()).astype(jnp.int32) if group != 8 else None
    if group == 8:
        where = [ORDER.index(m) for m in range(8)]
        order = jnp.array(where, jnp.int32)[
            lax.axis_index("kv").astype(jnp.int32) ^ jnp.arange(8, dtype=jnp.int32)
        ]
    source = jnp.concatenate([2 * order, 2 * order[::-1] + 1])

    angle = jnp.arange(length, dtype=F32)[:, None] * jnp.exp(
        jnp.arange(HEAD_DIM // 2, dtype=F32) * (-2.0 * math.log(10000.0) / HEAD_DIM)
    )
    cosine = jnp.cos(angle)
    sine = jnp.sin(angle)
    cosine = jnp.concatenate([cosine, cosine], axis=1)
    sine = jnp.concatenate([-sine, sine], axis=1)

    token_chunks = gather_chunks(flat16)
    all_tokens = jnp.concatenate(token_chunks, axis=0)
    dy_chunks = gather_chunks(after(dy16, *token_chunks[-2:]))
    dy_all = jnp.concatenate(dy_chunks, axis=0)
    normed = rms_norm(all_tokens.astype(F32), gains[0]).astype(BF16)
    normed = after(normed, *dy_chunks[-4:])
    qk = dot_plain(normed, w_three[:, : 2 * wide])
    v = dot_plain(normed, w_three[:, 2 * wide :]).astype(BF16)
    q, k, v, mass, mixed = attend_forward(source, first, qk, v, cosine, sine, doc_col, doc_row)

    def partial_hidden(start, stop):
        return dot_plain(chunk_rows(mixed, start, stop), out_w).astype(BF16)

    hidden = flat + scatter_rows(partial_hidden, [])

    second16 = rms_norm(hidden, gains[1]).astype(BF16)
    masses = lax.all_to_all(after(mass, second16).reshape(group, local), "kv", 0, 0)
    peak = jnp.max(jnp.sum(masses, axis=0)).reshape(1, 1)
    everyone = jnp.broadcast_to(peak, (ring * group, 1))
    summary = jnp.max(lax.all_to_all(everyone, ("seq", "kv"), 0, 0)).reshape(1)
    second_all = after(gather_rows(second16), summary)
    gate = dot_plain(second_all, gate_w)
    up = dot_plain(second_all, up_w)
    sig = jax.nn.sigmoid(gate)
    inner = (gate * sig * up).astype(BF16)
    grad_down = dot_left(dy_all, inner).astype(BF16)
    grads_down = lax.psum_scatter(grad_down, "seq", scatter_dimension=0, tiled=True)
    dinner = dot_right(after(dy_all, grad_down), down_w)
    dgate = (dinner * up * (sig * (1.0 + gate * (1.0 - sig)))).astype(BF16)
    dup = (dinner * (gate * sig)).astype(BF16)
    partials = []

    def partial_second(start, stop):
        partials.append(
            (
                dot_right(chunk_rows(dgate, start, stop), gate_w)
                + dot_right(chunk_rows(dup, start, stop), up_w)
            ).astype(BF16)
        )
        return partials[-1]

    grad_second = scatter_rows(partial_second, [])
    grads_gate = lax.psum_scatter(
        dot_left(after(second_all, *partials), dgate).astype(BF16), "seq", scatter_dimension=0, tiled=True
    )
    grad_hidden = dy16.astype(F32) + rms_back(hidden, gains[1], grad_second)
    dh_chunks = gather_chunks(after(grad_hidden.astype(BF16), grads_down))
    grads_down = grads_down.astype(F32).T
    dh_all = jnp.concatenate(dh_chunks, axis=0)

    def partial_result(start, stop):
        product = dot_plain(after(chunk_rows(inner, start, stop), *partials), down_w)
        return after(product.astype(BF16), *dh_chunks[-2:])

    ends, normed_parts = [], []
    result = hidden + scatter_rows(partial_result, ends)
    dmixed = dot_right(dh_all, out_w).astype(BF16)
    grad_w_out = dot_left(mixed, dh_all).astype(BF16)
    dqkv = attend_backward(source, last, q, k, v, dmixed, cosine, sine, doc_col, doc_row)

    def partial_normed(start, stop):
        product = dot_right(after(chunk_rows(dqkv, start, stop), grads_gate), w_three)
        normed_parts.append(product.astype(BF16))
        return normed_parts[-1]

    grad_normed = scatter_rows(partial_normed, ends)
    grad_input = grad_hidden + rms_back(flat, gains[0], grad_normed)

    grad_w_out = grad_w_out.reshape(mine, share, piece, width).transpose(1, 0, 2, 3)
    grad_w_out = lax.all_to_all(grad_w_out, "kv", 0, 0, axis_index_groups=pairs)
    grad_w_out = grad_w_out.reshape(ring * group * piece, width // group)
    grad_three = lax.psum_scatter(
        dot_left(normed, dqkv).astype(BF16), "seq", scatter_dimension=0, tiled=True
    )
    grads_up = dot_left(after(second_all, *normed_parts), dup).astype(BF16)
    grads_last = with_layout_constraint(
        jnp.concatenate([grads_up, grad_w_out], axis=1), Layout(major_to_minor=(0, 1))
    )
    grads_last = lax.psum_scatter(grads_last, "seq", scatter_dimension=0, tiled=True)
    grad_three = lax.all_to_all(grad_three.reshape(group, piece, 3 * wide), "kv", 0, 0)
    grad_three = grad_three.reshape(planes, share, piece, 3, mine, HEAD_DIM)
    grad_three = grad_three.transpose(3, 2, 1, 4, 0, 5).reshape(3, piece, width).astype(F32)

    scales = jnp.stack([gain_rows(flat, grad_normed), gain_rows(hidden, grad_second)], axis=1)
    scales = lax.all_to_all(scales.reshape(ring * group, piece, 2), ("seq", "kv"), 0, 0)
    scales = jnp.sum(scales, axis=0)

    early = (
        result.reshape(seqs, local, width).astype(BF16),
        grad_input.reshape(seqs, local, width),
        grad_three[0],
        grad_three[1],
        grad_three[2],
        scales[:, 0],
        scales[:, 1],
        grads_gate.astype(F32),
    )
    early, grads_last = lax.optimization_barrier((early, grads_last))
    grad_w_out = grads_last[:, units:].reshape(piece, width).astype(F32)
    grads_up = grads_last[:, :units].astype(F32)
    return early[:5] + (grad_w_out,) + early[5:8] + (grads_up, grads_down, summary)


def solution(mesh):
    tokens = P("seq", "kv", None)
    rows = P(("seq", "kv"), None)
    vector = P(("seq", "kv"))
    grid = P("seq", "kv")
    in_specs = (
        tokens, P("seq", "kv"), rows, rows, rows, rows, vector, vector, grid, grid,
        P("kv", "seq"), tokens,
    )
    out_specs = (
        tokens, tokens, rows, rows, rows, rows, vector, vector, grid, grid, P("kv", "seq"), P(),
    )
    return jax.shard_map(
        per_device, mesh=mesh, in_specs=in_specs, out_specs=out_specs, check_vma=False
    )
```

```python
import functools
import math

import jax
import jax.numpy as jnp
from jax import lax
from jax.experimental import pallas as pl
from jax.experimental.layout import Layout, with_layout_constraint
from jax.experimental.pallas import tpu as pltpu
from jax.sharding import PartitionSpec as P

HEAD_DIM = 128
EPSILON = 1e-05
BLOCK = 256
LOG2E = math.log2(math.e)
BF16 = jnp.bfloat16
F32 = jnp.float32


def dot_plain(left, right):
    return jnp.dot(left, right, preferred_element_type=F32)


def dot_left(left, right):
    return lax.dot_general(left, right, (((0,), (0,)), ((), ())), preferred_element_type=F32)


def dot_right(left, right):
    return lax.dot_general(left, right, (((1,), (1,)), ((), ())), preferred_element_type=F32)


def rms_norm(values, gain):
    return values * lax.rsqrt(jnp.mean(values * values, axis=-1, keepdims=True) + EPSILON) * gain


def rms_back(values, gain, grad):
    inverse = lax.rsqrt(jnp.mean(values * values, axis=-1, keepdims=True) + EPSILON)
    scaled = grad * gain
    moment = jnp.mean(values * scaled, axis=-1, keepdims=True)
    return inverse * scaled - values * (inverse * inverse * inverse) * moment


def gain_rows(values, grad):
    inverse = lax.rsqrt(jnp.mean(values * values, axis=-1, keepdims=True) + EPSILON)
    return jnp.sum(grad * values * inverse, axis=0)


ORDER = (0, 2, 4, 6, 1, 3, 5, 7)


def swap(values, mask):
    size = lax.axis_size("kv")
    return lax.ppermute(values, "kv", [(i, i ^ mask) for i in range(size)])


def owners():
    size = lax.axis_size("kv")
    if size == 8:
        return lax.axis_index("kv").astype(jnp.int32) ^ jnp.array(ORDER, jnp.int32)
    return jnp.arange(size, dtype=jnp.int32)


def gather_chunks(values):
    size = lax.axis_size("kv")
    if size != 8:
        return [lax.all_gather(values, "kv", axis=0, tiled=True)]
    half = values.shape[0] // 2
    near_x = swap(values, 2)
    near_y = swap(values, 4)
    core = swap(values, 1)
    far_top = swap(near_x[:half], 4)
    far_low = swap(near_y[half:], 2)
    core_x = swap(near_x, 1)
    core_y = swap(near_y, 1)
    core_top = swap(far_top, 1)
    core_low = swap(far_low, 1)
    return [values, near_x, near_y, far_top, far_low, core, core_x, core_y, core_top, core_low]


def gather_rows(values):
    return jnp.concatenate(gather_chunks(values), axis=0)


def add16(left, right):
    return (left.astype(F32) + right.astype(F32)).astype(BF16)


def scatter_rows(make, seen):
    size = lax.axis_size("kv")
    if size != 8:
        full = make(0, size)
        seen.append(full)
        return lax.psum_scatter(full, "kv", scatter_dimension=0, tiled=True).astype(F32)
    odd = make(4, 8)
    theirs = swap(odd, 1)
    even = make(0, 4)
    local = even.shape[0] // 4
    half = local // 2

    def both(chunk, low):
        rows = slice(chunk * local + low * half, chunk * local + (low + 1) * half)
        return add16(even[rows], theirs[rows])

    send_x, send_y = lax.optimization_barrier(
        (
            jnp.concatenate([both(1, 0), both(3, 0)], axis=0),
            jnp.concatenate([both(2, 1), both(3, 1)], axis=0),
        )
    )
    from_x, from_y = lax.optimization_barrier((swap(send_x, 2), swap(send_y, 4)))
    send_y, send_x = lax.optimization_barrier(
        (add16(both(2, 0), from_x[half:]), add16(both(1, 1), from_y[half:]))
    )
    last_y, last_x = lax.optimization_barrier((swap(send_y, 4), swap(send_x, 2)))
    seen += [last_y, last_x]
    top = both(0, 0).astype(F32) + from_x[:half].astype(F32) + last_y.astype(F32)
    low = both(0, 1).astype(F32) + from_y[:half].astype(F32) + last_x.astype(F32)
    return jnp.concatenate([top, low], axis=0)


def after(values, *others):
    return lax.optimization_barrier((values,) + tuple(others))[0]


def spread_small(values, axis):
    size = lax.axis_size(axis)
    return lax.all_to_all(jnp.broadcast_to(values[None], (size,) + values.shape), axis, 0, 0)


def turn(values, cosine, sine):
    return values * cosine + pltpu.roll(values, HEAD_DIM // 2, 1) * sine


def forward_kernel(
    heads, parts, length, scale, offset,
    source, first, qk_hbm, v_hbm, cos_ref, sin_ref, doc_col, doc_row,
    q_ref, k_ref, v_ref, mass_ref, mixed_hbm,
    qk_s, mixed_s, sems,
):
    wide = heads * HEAD_DIM
    rows = length // parts

    def load(b):
        start = pl.multiple_of(source[b] * rows, rows)
        here = pl.ds(b * rows, rows)
        return (
            pltpu.make_async_copy(qk_hbm.at[pl.ds(start, rows), :], qk_s.at[here, :], sems.at[0, b]),
            pltpu.make_async_copy(v_hbm.at[pl.ds(start, rows), :], v_ref.at[here, :], sems.at[1, b]),
        )

    def store(b):
        start = pl.multiple_of(source[b] * rows, rows)
        return pltpu.make_async_copy(
            mixed_s.at[pl.ds(b * rows, rows), :], mixed_hbm.at[pl.ds(start, rows), :], sems.at[2, b]
        )

    for b in range(parts):
        for copy in load(b):
            copy.start()
    for b in range(parts):
        for copy in load(b):
            copy.wait()

    def rope(b, carry):
        here = pl.ds(pl.multiple_of(b * BLOCK, BLOCK), BLOCK)
        cosine = cos_ref[here, :]
        sine = sin_ref[here, :]
        for h in range(heads):
            lanes = slice(h * HEAD_DIM, (h + 1) * HEAD_DIM)
            more = slice(wide + h * HEAD_DIM, wide + (h + 1) * HEAD_DIM)
            q_ref[here, lanes] = turn(qk_s[here, lanes], cosine, sine).astype(BF16)
            k_ref[here, lanes] = turn(qk_s[here, more], cosine, sine).astype(BF16)
        return carry

    lax.fori_loop(0, length // BLOCK, rope, 0)

    def query_block(i, carry):
        here = pl.ds(pl.multiple_of(i * BLOCK, BLOCK), BLOCK)
        docs = doc_col[here, :]
        row = lax.broadcasted_iota(jnp.int32, (BLOCK, BLOCK), 0)
        col = lax.broadcasted_iota(jnp.int32, (BLOCK, BLOCK), 1)

        def key_block(j, carry):
            accs, mass = carry
            there = pl.ds(pl.multiple_of(j * BLOCK, BLOCK), BLOCK)
            allowed = (docs == doc_row[:, there]) & (row + (i - j) * BLOCK >= col)
            out = []
            for h in range(heads):
                lanes = slice(h * HEAD_DIM, (h + 1) * HEAD_DIM)
                score = dot_right(q_ref[here, lanes], k_ref[there, lanes])
                prob = 1.0 / (1.0 + jnp.exp2(score * (-scale * LOG2E) + offset * LOG2E))
                prob = jnp.where(allowed, prob, 0.0)
                for part in range(BLOCK // 128):
                    mass = mass + prob[:, part * 128 : (part + 1) * 128]
                out.append(accs[h] + dot_plain(prob.astype(BF16), v_ref[there, lanes]))
            return (tuple(out), mass)

        zero = jnp.zeros((BLOCK, HEAD_DIM), F32)
        accs, mass = lax.fori_loop(first[i], i + 1, key_block, ((zero,) * heads, zero))
        for h in range(heads):
            mixed_s[here, h * HEAD_DIM : (h + 1) * HEAD_DIM] = accs[h].astype(BF16)
        mass_ref[here, :] = jnp.sum(mass, axis=1, keepdims=True)
        return carry

    lax.fori_loop(0, length // BLOCK, query_block, 0)
    for b in range(parts):
        store(b).start()
    for b in range(parts):
        store(b).wait()


def attend_forward(source, first, qk, v, cosine, sine, doc_col, doc_row):
    length, wide = v.shape
    heads = wide // HEAD_DIM
    parts = source.shape[0]
    vmem = pl.BlockSpec(memory_space=pltpu.VMEM)
    smem = pl.BlockSpec(memory_space=pltpu.SMEM)
    hbm = pl.BlockSpec(memory_space=pl.ANY)
    same = jax.ShapeDtypeStruct((length, wide), BF16)
    return pl.pallas_call(
        functools.partial(
            forward_kernel, heads, parts, length, 1.0 / math.sqrt(HEAD_DIM), math.log(length)
        ),
        name="attend_forward",
        out_shape=(same, same, same, jax.ShapeDtypeStruct((length, 1), F32), same),
        in_specs=[smem, smem, hbm, hbm, vmem, vmem, vmem, vmem],
        out_specs=(vmem, vmem, vmem, vmem, hbm),
        scratch_shapes=[
            pltpu.VMEM((length, 2 * wide), F32),
            pltpu.VMEM((length, wide), BF16),
            pltpu.SemaphoreType.DMA((3, parts)),
        ],
        cost_estimate=pl.CostEstimate(
            flops=2 * length * length * wide,
            transcendentals=length * length * heads,
            bytes_accessed=length * wide * 18,
        ),
    )(source, first, qk, v, cosine, sine, doc_col, doc_row)


def backward_kernel(
    heads, parts, length, scale, offset,
    source, last, q_ref, k_ref, v_ref, g_hbm, cos_ref, sin_ref, doc_col, doc_row,
    out_hbm,
    g_s, dq_s, out_s, sems,
):
    wide = heads * HEAD_DIM
    rows = length // parts

    def load(b):
        start = pl.multiple_of(source[b] * rows, rows)
        return pltpu.make_async_copy(
            g_hbm.at[pl.ds(start, rows), :], g_s.at[pl.ds(b * rows, rows), :], sems.at[0, b]
        )

    def store(b):
        start = pl.multiple_of(source[b] * rows, rows)
        return pltpu.make_async_copy(
            out_s.at[pl.ds(b * rows, rows), :], out_hbm.at[pl.ds(start, rows), :], sems.at[1, b]
        )

    for b in range(parts):
        load(b).start()
    dq_s[...] = jnp.zeros_like(dq_s)
    for b in range(parts):
        load(b).wait()

    def key_block(j, carry):
        there = pl.ds(pl.multiple_of(j * BLOCK, BLOCK), BLOCK)
        docs = doc_col[there, :]
        row = lax.broadcasted_iota(jnp.int32, (BLOCK, BLOCK), 0)
        col = lax.broadcasted_iota(jnp.int32, (BLOCK, BLOCK), 1)

        def query_block(i, carry):
            dks, dvs = carry
            here = pl.ds(pl.multiple_of(i * BLOCK, BLOCK), BLOCK)
            allowed = (docs == doc_row[:, here]) & (col + (i - j) * BLOCK >= row)
            new_k, new_v = [], []
            for h in range(heads):
                lanes = slice(h * HEAD_DIM, (h + 1) * HEAD_DIM)
                query = q_ref[here, lanes]
                grad = g_s[here, lanes]
                score = dot_right(k_ref[there, lanes], query)
                prob = 1.0 / (1.0 + jnp.exp2(score * (-scale * LOG2E) + offset * LOG2E))
                prob = jnp.where(allowed, prob, 0.0)
                new_v.append(dvs[h] + dot_plain(prob.astype(BF16), grad))
                dprob = dot_right(v_ref[there, lanes], grad)
                dscore = (dprob * (prob - prob * prob)).astype(BF16)
                new_k.append(dks[h] + dot_plain(dscore, query))
                dq_s[here, lanes] += dot_left(dscore, k_ref[there, lanes])
            return (tuple(new_k), tuple(new_v))

        zero = (jnp.zeros((BLOCK, HEAD_DIM), F32),) * heads
        dks, dvs = lax.fori_loop(j, last[j], query_block, (zero, zero))
        cosine = cos_ref[there, :]
        sine = sin_ref[there, :]
        for h in range(heads):
            lanes = slice(h * HEAD_DIM, (h + 1) * HEAD_DIM)
            more = slice(wide + h * HEAD_DIM, wide + (h + 1) * HEAD_DIM)
            most = slice(2 * wide + h * HEAD_DIM, 2 * wide + (h + 1) * HEAD_DIM)
            out_s[there, lanes] = turn(dq_s[there, lanes] * scale, cosine, -sine).astype(BF16)
            out_s[there, more] = turn(dks[h] * scale, cosine, -sine).astype(BF16)
            out_s[there, most] = dvs[h].astype(BF16)
        return carry

    lax.fori_loop(0, length // BLOCK, key_block, 0)
    for b in range(parts):
        store(b).start()
    for b in range(parts):
        store(b).wait()


def attend_backward(source, last, q, k, v, grad, cosine, sine, doc_col, doc_row):
    length, wide = v.shape
    heads = wide // HEAD_DIM
    parts = source.shape[0]
    vmem = pl.BlockSpec(memory_space=pltpu.VMEM)
    smem = pl.BlockSpec(memory_space=pltpu.SMEM)
    hbm = pl.BlockSpec(memory_space=pl.ANY)
    return pl.pallas_call(
        functools.partial(
            backward_kernel, heads, parts, length, 1.0 / math.sqrt(HEAD_DIM), math.log(length)
        ),
        name="attend_backward",
        out_shape=jax.ShapeDtypeStruct((length, 3 * wide), BF16),
        in_specs=[smem, smem, vmem, vmem, vmem, hbm, vmem, vmem, vmem, vmem],
        out_specs=hbm,
        scratch_shapes=[
            pltpu.VMEM((length, wide), BF16),
            pltpu.VMEM((length, wide), F32),
            pltpu.VMEM((length, 3 * wide), BF16),
            pltpu.SemaphoreType.DMA((2, parts)),
        ],
        cost_estimate=pl.CostEstimate(
            flops=5 * length * length * wide,
            transcendentals=length * length * heads,
            bytes_accessed=length * wide * 14,
        ),
    )(source, last, q, k, v, grad, cosine, sine, doc_col, doc_row)


def per_device(
    tokens,
    doc_ids,
    w_query,
    w_key,
    w_value,
    w_out,
    gain_attn,
    gain_ffn,
    w_gate,
    w_up,
    w_down,
    cotangent,
):
    ring = lax.axis_size("seq")
    group = lax.axis_size("kv")
    seqs, local, width = tokens.shape
    length = local * group
    piece = w_query.shape[0]
    heads = width // HEAD_DIM
    planes = heads // ring
    share = group // planes
    mine = ring // share
    wide = mine * HEAD_DIM
    pairs = [[j * share + c for c in range(share)] for j in range(planes)]

    def chunk_rows(values, start, stop):
        return values[start * local : stop * local]

    flat16 = tokens.reshape(local, width)
    flat = flat16.astype(F32)
    dy16 = cotangent.reshape(local, width)

    w_three = jnp.stack([w_query, w_key, w_value])
    w_three = w_three.reshape(3, piece, share, mine, planes, HEAD_DIM)
    w_three = w_three.transpose(4, 2, 1, 0, 3, 5).reshape(group, piece, 3 * wide)
    w_three = lax.all_to_all(w_three, "kv", 0, 0).reshape(group * piece, 3 * wide)
    w_three = lax.all_gather(w_three, "seq", axis=0, tiled=True)
    out_w = lax.all_gather(w_out, "seq", axis=0, tiled=False)
    out_w = lax.all_to_all(
        out_w.reshape(share, mine, piece, width), "kv", 0, 0, axis_index_groups=pairs
    )
    out_w = out_w.transpose(1, 0, 2, 3).reshape(wide, width)
    units = w_gate.shape[1]
    gate_up_w = jnp.concatenate([w_gate, w_up], axis=1)
    gate_up_w = lax.all_gather(gate_up_w, "seq", axis=0, tiled=True)
    gate_w, up_w = gate_up_w[:, :units], gate_up_w[:, units:]
    down_w = lax.all_gather(w_down, "seq", axis=1, tiled=True)

    gains = spread_small(spread_small(jnp.stack([gain_attn, gain_ffn]), "kv"), "seq")
    gains = gains.transpose(2, 0, 1, 3).reshape(2, width).astype(F32)
    ids = spread_small(doc_ids.reshape(local), "kv")

    half = local // 2
    by_pos = jnp.concatenate([ids[:, :half], ids[::-1, half:]], axis=0).reshape(length)
    blocks = length // BLOCK
    starts = by_pos.reshape(blocks, BLOCK)[:, 0]
    ends = by_pos.reshape(blocks, BLOCK)[:, -1]
    first = jnp.sum((by_pos[None] < starts[:, None]).astype(jnp.int32), axis=1) // BLOCK
    last = (jnp.sum((by_pos[None] <= ends[:, None]).astype(jnp.int32), axis=1) + BLOCK - 1) // BLOCK
    doc_col = by_pos.reshape(length, 1)
    doc_row = by_pos.reshape(1, length)
    order = jnp.argsort(owners()).astype(jnp.int32) if group != 8 else None
    if group == 8:
        where = [ORDER.index(m) for m in range(8)]
        order = jnp.array(where, jnp.int32)[
            lax.axis_index("kv").astype(jnp.int32) ^ jnp.arange(8, dtype=jnp.int32)
        ]
    source = jnp.concatenate([2 * order, 2 * order[::-1] + 1])

    angle = jnp.arange(length, dtype=F32)[:, None] * jnp.exp(
        jnp.arange(HEAD_DIM // 2, dtype=F32) * (-2.0 * math.log(10000.0) / HEAD_DIM)
    )
    cosine = jnp.cos(angle)
    sine = jnp.sin(angle)
    cosine = jnp.concatenate([cosine, cosine], axis=1)
    sine = jnp.concatenate([-sine, sine], axis=1)

    token_chunks = gather_chunks(flat16)
    all_tokens = jnp.concatenate(token_chunks, axis=0)
    dy_chunks = gather_chunks(after(dy16, *token_chunks[-2:]))
    dy_all = jnp.concatenate(dy_chunks, axis=0)
    normed = rms_norm(all_tokens.astype(F32), gains[0]).astype(BF16)
    normed = after(normed, *dy_chunks[-4:])
    qk = dot_plain(normed, w_three[:, : 2 * wide])
    v = dot_plain(normed, w_three[:, 2 * wide :]).astype(BF16)
    q, k, v, mass, mixed = attend_forward(source, first, qk, v, cosine, sine, doc_col, doc_row)

    def partial_hidden(start, stop):
        return dot_plain(chunk_rows(mixed, start, stop), out_w).astype(BF16)

    hidden = flat + scatter_rows(partial_hidden, [])

    second16 = rms_norm(hidden, gains[1]).astype(BF16)
    masses = lax.all_to_all(after(mass, second16).reshape(group, local), "kv", 0, 0)
    peak = jnp.max(jnp.sum(masses, axis=0)).reshape(1, 1)
    everyone = jnp.broadcast_to(peak, (ring * group, 1))
    summary = jnp.max(lax.all_to_all(everyone, ("seq", "kv"), 0, 0)).reshape(1)
    second_all = after(gather_rows(second16), summary)
    gate = dot_plain(second_all, gate_w)
    up = dot_plain(second_all, up_w)
    sig = jax.nn.sigmoid(gate)
    inner = (gate * sig * up).astype(BF16)
    grad_down = dot_left(dy_all, inner).astype(BF16)
    grads_down = lax.psum_scatter(grad_down, "seq", scatter_dimension=0, tiled=True)
    dinner = dot_right(after(dy_all, grad_down), down_w)
    dgate = (dinner * up * (sig * (1.0 + gate * (1.0 - sig)))).astype(BF16)
    dup = (dinner * (gate * sig)).astype(BF16)
    partials = []

    def partial_second(start, stop):
        partials.append(
            (
                dot_right(chunk_rows(dgate, start, stop), gate_w)
                + dot_right(chunk_rows(dup, start, stop), up_w)
            ).astype(BF16)
        )
        return partials[-1]

    grad_second = scatter_rows(partial_second, [])
    grads_gate = lax.psum_scatter(
        dot_left(after(second_all, *partials), dgate).astype(BF16), "seq", scatter_dimension=0, tiled=True
    )
    grad_hidden = dy16.astype(F32) + rms_back(hidden, gains[1], grad_second)
    dh_chunks = gather_chunks(after(grad_hidden.astype(BF16), grads_down))
    grads_down = grads_down.astype(F32).T
    dh_all = jnp.concatenate(dh_chunks, axis=0)

    def partial_result(start, stop):
        product = dot_plain(after(chunk_rows(inner, start, stop), *partials), down_w)
        return after(product.astype(BF16), *dh_chunks[-2:])

    ends, normed_parts = [], []
    result = hidden + scatter_rows(partial_result, ends)
    dmixed = dot_right(dh_all, out_w).astype(BF16)
    grad_w_out = dot_left(mixed, dh_all).astype(BF16)
    dqkv = attend_backward(source, last, q, k, v, dmixed, cosine, sine, doc_col, doc_row)

    def partial_normed(start, stop):
        product = dot_right(after(chunk_rows(dqkv, start, stop), grads_gate), w_three)
        normed_parts.append(product.astype(BF16))
        return normed_parts[-1]

    grad_normed = scatter_rows(partial_normed, ends)
    grad_input = grad_hidden + rms_back(flat, gains[0], grad_normed)

    grad_w_out = grad_w_out.reshape(mine, share, piece, width).transpose(1, 0, 2, 3)
    grad_w_out = lax.all_to_all(grad_w_out, "kv", 0, 0, axis_index_groups=pairs)
    grad_w_out = grad_w_out.reshape(ring, -1, units)
    grad_three = lax.psum_scatter(
        dot_left(normed, dqkv).astype(BF16), "seq", scatter_dimension=0, tiled=True
    )
    grads_up = dot_left(after(second_all, *normed_parts), dup).astype(BF16)
    grads_last = with_layout_constraint(
        jnp.concatenate([grads_up.reshape(ring, -1, units), grad_w_out], axis=1).reshape(-1, units),
        Layout(major_to_minor=(0, 1)),
    )
    grads_last = lax.psum_scatter(grads_last, "seq", scatter_dimension=0, tiled=True)
    grad_three = lax.all_to_all(grad_three.reshape(group, piece, 3 * wide), "kv", 0, 0)
    grad_three = grad_three.reshape(planes, share, piece, 3, mine, HEAD_DIM)
    grad_three = grad_three.transpose(3, 2, 1, 4, 0, 5).reshape(3, piece, width).astype(F32)

    scales = jnp.stack([gain_rows(flat, grad_normed), gain_rows(hidden, grad_second)], axis=1)
    scales = lax.all_to_all(scales.reshape(ring * group, piece, 2), ("seq", "kv"), 0, 0)
    scales = jnp.sum(scales, axis=0)

    early = (
        result.reshape(seqs, local, width).astype(BF16),
        grad_input.reshape(seqs, local, width),
        grad_three[0],
        grad_three[1],
        grad_three[2],
        scales[:, 0],
        scales[:, 1],
        grads_gate.astype(F32),
    )
    early, grads_last = lax.optimization_barrier((early, grads_last))
    rows = grads_gate.shape[0]
    grad_w_out = grads_last[rows:].reshape(piece, width).astype(F32)
    grads_up = grads_last[:rows].astype(F32)
    return early[:5] + (grad_w_out,) + early[5:8] + (grads_up, grads_down, summary)


def solution(mesh):
    tokens = P("seq", "kv", None)
    rows = P(("seq", "kv"), None)
    vector = P(("seq", "kv"))
    grid = P("seq", "kv")
    in_specs = (
        tokens, P("seq", "kv"), rows, rows, rows, rows, vector, vector, grid, grid,
        P("kv", "seq"), tokens,
    )
    out_specs = (
        tokens, tokens, rows, rows, rows, rows, vector, vector, grid, grid, P("kv", "seq"), P(),
    )
    return jax.shard_map(
        per_device, mesh=mesh, in_specs=in_specs, out_specs=out_specs, check_vma=False
    )
```
